128 devices in a mesh: grp: 4 (over z), rve: 32 (over y, x, core).
Axes of the slice: x: 4, y: 4, z: 4, core: 2. Of those that a mesh axis runs over, the one named last changes fastest.
Arguments:
- displacement: float32 [3, 256, 32, 128], P(None, ('grp', 'rve')), may hold values from -6 to 6
- stiffness: bfloat16 [27, 3, 3, 256, 32, 128], P(None, None, None, ('grp', 'rve')), may hold values from -0.65625 to 0.65625
- external: float32 [3, 256, 32, 128], P(None, ('grp', 'rve')), may hold values from -6 to 6
- point_node: int32 [8], P('grp'), may hold values from 0 to 262143
- point_owner: int32 [8, 1], P('grp'), may hold values from 0 to 3; in each aligned block of 2 rows (0 to 1, 2 to 3, ...) no two rows name the same one
- point_load: float32 [8, 18], P('grp'), may hold values from -6 to 6
- moduli_diag: float32 [4, 6, 32, 64, 128], P('grp', None, 'rve'), may hold values from 1.5 to 4
- moduli_off: float32 [4, 36, 32, 64, 128], P('grp', None, 'rve'), may hold values from -1 to 1
- schmid: float32 [4, 72, 32, 64, 128], P('grp', None, 'rve'), may hold values from -1 to 1
- crss: float32 [4, 12, 32, 64, 128], P('grp', None, 'rve'), may hold values from 0.3 to 3
- branch: int32 [4, 32, 64, 128], P('grp', 'rve'), may hold values from 0 to 4095
- rate: float32 [4, 32, 64, 128], P('grp', 'rve'), may hold values from 0.03 to 0.3
Outputs:
- residual: float32 [3, 256, 32, 128], P(None, ('grp', 'rve'))
- point_stress: float32 [8, 6], P('grp')
The draws below stay inside these ranges and needn't reach their ends.
Inputs may be any that keep to these rules, and one draw needn't show every extreme that they name: `point_owner`: among the 2 points of one quarter's list, at most 1 name the same volume, a bound that some block reaches.
All inputs are finite; a program needn't handle non-finite values.
Results may differ from the reference program's by a relative error of at most 0.0003.
Values sent between devices are 32-bit elements; how exact they have to be, the bound alone decides.
No kernel may reach another device: no remote copies, remote signals or barrier semaphores. Data moves between devices by JAX's collectives and lax.ppermute only.
A program may use at most 128 MiB of HBM per device.

```python
import math
import jax
import jax.numpy as jnp
import numpy as np
from jax import lax

XD = 2
NY = 32
NZ = 128
P_Q = 2
VY = 64
VZ = 128
SLIP = 12
SWEEPS = 10
CAP = 1
NX = 256
P_TOTAL = 8
VOX = 32
N_GRP = 4
N_RVE = 32


def set_ends(entries, own_key, smallest, top_value):
    place = [jax.random.randint(jax.random.fold_in(own_key, axis), (), 0, length) for axis, length in enumerate(entries.shape)]
    longest = entries.shape.index(max(entries.shape))
    neighbour = place[:longest] + [(place[longest] + 1) % entries.shape[longest]] + place[longest + 1:]
    return entries.at[tuple(place)].set(smallest).at[tuple(neighbour)].set(top_value)


def levels(key, shape, pieces, smallest, top_value):
    gain = 1.0
    for axis_at, shards_of in pieces:
        draws = jax.random.uniform(jax.random.fold_in(jax.random.fold_in(key, 6), axis_at), (shards_of,), jnp.float32, smallest / len(pieces), top_value / len(pieces))
        gain = gain * jnp.repeat(jnp.exp(draws), shape[axis_at] // shards_of).reshape((-1,) + (1,) * (len(shape) - 1 - axis_at))
    return gain


def routed_block(key, own, number, rows, number_of, top, limit, lean):
    ranking = jax.random.permutation(key, number_of)
    crowded, usual = shares(number_of, rows * top, limit, lean, True), shares(number_of, rows * top, limit, lean, False)
    places = jnp.arange(number_of)

    def named(sizes, rotation):
        used = int((sizes > 0).sum())
        fixed = max(1, used // 4)
        passed = fixed + (places - fixed + rotation * (used - fixed)) % max(1, number_of - fixed)
        return jnp.zeros((number_of,), jnp.int32).at[ranking[jnp.where(places < fixed, places, passed)]].set(jnp.asarray(sizes, jnp.int32))

    sizes = jnp.where(number % 4 == 0, named(crowded, number // 4), named(usual, number - number // 4 - 1))
    mixed = jax.random.permutation(jax.random.fold_in(own, 3), number_of)
    donor, sink = mixed[0:number_of // 2 * 2:2], mixed[1:number_of // 2 * 2:2]
    room = jnp.minimum(sizes[donor] - 1, limit - sizes[sink]) // 2
    room = jnp.where((donor == ranking[0]) | (sink == ranking[0]) | (sizes[sink] == 0), 0, jnp.maximum(room, 0))
    passed = jax.random.randint(jax.random.fold_in(own, 4), (number_of // 2,), 0, 1 << 20) % (room + 1)
    sizes = sizes.at[donor].add(-passed).at[sink].add(passed)
    items = jnp.searchsorted(jnp.cumsum(sizes), jnp.arange(rows * top), side="right").astype(jnp.int32)
    table = items.reshape(top, rows).T
    table = table[jax.random.permutation(jax.random.fold_in(own, 1), rows)]
    rotation = jax.random.randint(jax.random.fold_in(own, 2), (rows, 1), 0, top)
    return jnp.take_along_axis(table, (jnp.arange(top)[None, :] + rotation) % top, axis=1)


def shares(number_of, total, most, lean, full):
    weights = [(1 << 20) // math.isqrt(grade ** lean) + 1 for grade in range(1, number_of + 1)]
    largest = most if full else min(most, max(-(-total // number_of), total * weights[0] // sum(weights)))
    least = 1 if total - largest >= number_of - 1 else 0
    given, rest = [largest] + [least] * (number_of - 1), total - largest - least * (number_of - 1)
    while rest > 0:
        free = [i for i in range(1, number_of) if given[i] < largest] or [i for i in range(1, number_of) if given[i] < most]
        pool, left = sum([weights[i] for i in free]), rest
        for i in free:
            more = min(most - given[i], max(1, left * weights[i] // pool), rest)
            given[i] = given[i] + more
            rest = rest - more
    return np.array(given)


def scatter_about(own_key, shape, scale, limit, cuts=(), held_as=jnp.bfloat16):
    entries = jax.random.normal(own_key, shape, jnp.float32) * scale
    if len(cuts) > 0:
        entries = levels(own_key, shape, cuts, -0.22, 0.18) * entries
    return jnp.clip(entries, min=-limit, max=limit).astype(held_as)


def setup_inputs(seed: int = 0) -> dict:
    seeds = jax.random.split(jax.random.key(seed), 13)
    displacement = scatter_about(seeds[0], (3, NX, NY, NZ), 1.0, 6.0, ((1, 128),), jnp.float32)
    stiffness = scatter_about(seeds[1], (27, 3, 3, NX, NY, NZ), 0.11, 0.65625, ((3, 128),))
    external = scatter_about(seeds[2], (3, NX, NY, NZ), 1.0, 6.0, ((1, 128),), jnp.float32)
    point_node = set_ends(jax.random.randint(seeds[3], (P_TOTAL,), 0, XD * N_RVE * NY * NZ), jax.random.fold_in(seeds[3], 1), 0, (XD * N_RVE * NY * NZ) - 1).astype(jnp.int32)
    point_owner_keys = jax.random.split(jax.random.fold_in(seeds[4], 1), P_TOTAL // P_Q)
    point_owner_turns = jax.random.permutation(jax.random.fold_in(seeds[4], 3), P_TOTAL // P_Q)
    point_owner = jax.vmap(lambda own, number: routed_block(jax.random.fold_in(seeds[4], 2), own, number, P_Q, N_GRP, 1, CAP, 2))(point_owner_keys, point_owner_turns).reshape((P_TOTAL, 1))
    point_load = scatter_about(seeds[5], (P_TOTAL, 18), 1 ** -0.5, 6.0, ((0, 4),), jnp.float32)
    moduli_diag = jnp.clip(jnp.exp(math.log(4.0) - 0.98082925 * jax.random.uniform(seeds[6], (N_GRP, 6, VOX, VY, VZ), jnp.float32) ** levels(seeds[6], (N_GRP, 6, VOX, VY, VZ), ((0, 4), (2, 32)), -0.2, 0.2)), 1.5, 4.0)
    moduli_off = scatter_about(seeds[7], (N_GRP, 36, VOX, VY, VZ), 0.2, 1.0, ((0, 4), (2, 32)), jnp.float32)
    schmid = scatter_about(seeds[8], (N_GRP, 72, VOX, VY, VZ), 0.25, 1.0, ((0, 4), (2, 32)), jnp.float32)
    crss = jnp.clip(jnp.exp(math.log(3.0) - 2.3025851 * jax.random.uniform(seeds[9], (N_GRP, 12, VOX, VY, VZ), jnp.float32) ** levels(seeds[9], (N_GRP, 12, VOX, VY, VZ), ((0, 4), (2, 32)), -0.2, 0.2)), 0.3, 3.0)
    branch = set_ends(jax.random.randint(seeds[10], (N_GRP, VOX, VY, VZ), 0, 4096), jax.random.fold_in(seeds[10], 1), 0, 4095).astype(jnp.int32)
    rate = jnp.clip(jnp.exp(math.log(0.3) - 2.3025852 * jax.random.uniform(seeds[11], (N_GRP, VOX, VY, VZ), jnp.float32) ** levels(seeds[11], (N_GRP, VOX, VY, VZ), ((0, 4), (1, 32)), -0.2, 0.2)), 0.03, 0.3)
    return dict(displacement=displacement, stiffness=stiffness, external=external, point_node=point_node, point_owner=point_owner, point_load=point_load, moduli_diag=moduli_diag, moduli_off=moduli_off, schmid=schmid, crss=crss, branch=branch, rate=rate)


RELAX = 0.15
NEIGHBOUR_WEIGHT = 1.0 / 6.0


def stiff_apply(blocks, padded):
    extent = (padded.shape[1] - 2, padded.shape[2] - 2, padded.shape[3] - 2)
    summed = jnp.zeros((3,) + extent, jnp.float32)
    for i in range(3):
        for j in range(3):
            for k in range(3):
                offset = i * 9 + j * 3 + k
                window = padded[:, i:i + extent[0], j:j + extent[1], k:k + extent[2]]
                summed = summed + jnp.sum(blocks[offset].astype(jnp.float32) * window[None], axis=1)
    return summed


def node_strain(padded):
    extent = (padded.shape[1] - 2, padded.shape[2] - 2, padded.shape[3] - 2)

    def gradient(c, k):
        lower = [slice(1, 1 + extent[0]), slice(1, 1 + extent[1]), slice(1, 1 + extent[2])]
        upper = list(lower)
        lower[k] = slice(0, extent[k])
        upper[k] = slice(2, 2 + extent[k])
        return (padded[c][tuple(upper)] - padded[c][tuple(lower)]) * 0.5

    table = [[gradient(c, k) for k in range(3)] for c in range(3)]
    return jnp.stack([table[0][0], table[1][1], table[2][2], table[1][2] + table[2][1],
                      table[0][2] + table[2][0], table[0][1] + table[1][0]])


def activity(branch):
    bit_index = jnp.arange(SLIP, dtype=jnp.int32)
    return (jnp.right_shift(branch[None], bit_index[:, None, None, None]) & 1).astype(jnp.float32)


def make_entry(diagonal, offdiag, schmid_rows, critical, plastic_rate):
    matrix = offdiag.reshape((6, 6) + offdiag.shape[1:]) + jnp.eye(6, dtype=jnp.float32)[:, :, None, None, None] * diagonal[None]
    schmid_mat = schmid_rows.reshape((12, 6) + schmid_rows.shape[1:])
    return (matrix, schmid_mat, critical[:, None], plastic_rate[:, None], jnp.swapaxes(schmid_mat, 0, 1))


def contract(matrix, field):
    summed = matrix[:, 0][:, None] * field[0][None]
    for j in range(1, matrix.shape[1]):
        summed = summed + matrix[:, j][:, None] * field[j][None]
    return summed


def sweeps(ebar, entry, plane_sum):
    baseline = ebar[:, :, None, None, None]
    matrix, schmid_mat, critical, plastic_rate, schmid_back = entry
    shape = (6, ebar.shape[1]) + matrix.shape[2:]
    fluctuation = jnp.zeros(shape, jnp.float32)
    plastic = jnp.zeros(shape, jnp.float32)
    for sweep in range(SWEEPS):
        strain = baseline + fluctuation - plastic
        stress = contract(matrix, strain)
        resolved = contract(schmid_mat, stress)
        slipped = plastic_rate * (resolved - critical * jnp.tanh(resolved / critical))
        plastic = plastic + contract(schmid_back, slipped)
        beside = plane_sum(strain, stress) + jnp.roll(stress, 1, axis=3) + jnp.roll(stress, -1, axis=3)
        beside = beside + jnp.roll(stress, 1, axis=4) + jnp.roll(stress, -1, axis=4)
        fluctuation = fluctuation - RELAX * (stress - NEIGHBOUR_WEIGHT * beside)
    final_strain = baseline + fluctuation - plastic
    return contract(matrix, final_strain)


def roll_planes(strain, stress):
    return jnp.roll(stress, 1, axis=2) + jnp.roll(stress, -1, axis=2)


def reference(displacement, stiffness, external, point_node, point_owner, point_load, moduli_diag, moduli_off, schmid, crss, branch, rate):
    padded = jnp.pad(displacement, ((0, 0), (1, 1), (1, 1), (1, 1)))
    applied = stiff_apply(stiffness, padded)
    strain_field = node_strain(padded).reshape(6, -1)
    quarter_of = (jnp.arange(P_TOTAL, dtype=jnp.int32) // P_Q).astype(jnp.int32)
    flat_node = (quarter_of * (XD * N_RVE * NY * NZ) + point_node).astype(jnp.int32)
    ebar = strain_field[:, flat_node].T

    def one_point(inputs):
        strain_point, owner_id = inputs
        plastic_rate = activity(branch[owner_id]) * rate[owner_id]
        entry = make_entry(moduli_diag[owner_id], moduli_off[owner_id], schmid[owner_id], crss[owner_id], plastic_rate)
        final = sweeps(strain_point[:, None], entry, roll_planes)
        return jnp.sum(final, axis=(1, 2, 3, 4)) / (VOX * VY * VZ)

    point_stress = lax.map(one_point, (ebar, point_owner[:, 0]))
    force = jnp.einsum("pcj,pj->pc", point_load.reshape(-1, 3, 6), point_stress, precision=lax.Precision.HIGHEST)
    flat = (external - applied).reshape(3, -1).at[:, flat_node].add(-force.T)
    return flat.reshape(external.shape), point_stress
```

```python
import jax
import jax.numpy as jnp
from jax import lax
from jax.experimental import pallas as pl
from jax.experimental.pallas import tpu as pltpu
from jax.sharding import PartitionSpec as P

SLIP = 12
RELAX = 0.15
SHARE = RELAX / 6.0
ROWS = 64
LANES = 128
SLOTS = 2
FIELDS = SLOTS * 6
VMEM_LIMIT = 56 * 1024 * 1024
F32 = jnp.float32

VM = pl.BlockSpec(memory_space=pltpu.VMEM)
SM = pl.BlockSpec(memory_space=pltpu.SMEM)


def call(kernel, name, in_specs, outs, scratch=(), out_specs=None):
    return pl.pallas_call(
        kernel,
        name=name,
        in_specs=in_specs,
        out_specs=[VM] * len(outs) if out_specs is None else out_specs,
        out_shape=[jax.ShapeDtypeStruct(s, F32) for s in outs],
        scratch_shapes=list(scratch),
        compiler_params=pltpu.CompilerParams(vmem_limit_bytes=VMEM_LIMIT),
    )


def chunks(body):
    def step(k, carry):
        body(pl.ds(pl.multiple_of(k * 8, 8), 8))
        return carry

    lax.fori_loop(0, ROWS // 8, step, 0)


def pack_kernel(diag, off, schmid, crss, branch, rate, c_ref, s_ref):
    for i in range(6):
        for j in range(6):
            v = off[6 * i + j]
            c_ref[6 * i + j] = v + diag[i] if i == j else v
    bits = branch[...]
    speed = rate[...]
    for a in range(SLIP):
        limit = crss[a]
        inverse = 1.0 / limit
        for j in range(6):
            s_ref[6 * a + j] = schmid[6 * a + j] * inverse
        active = (jnp.right_shift(bits, a) & 1).astype(F32)
        s_ref[6 * SLIP + a] = active * speed * (limit * limit)


def pack(diag, off, schmid, crss, branch, rate):
    block = lambda n: pl.BlockSpec((n, 8, LANES), lambda k: (0, k, 0))
    flat = pl.BlockSpec((8, LANES), lambda k: (k, 0))
    return pl.pallas_call(
        pack_kernel,
        name="pack",
        grid=(ROWS // 8,),
        in_specs=[block(6), block(36), block(72), block(12), flat, flat],
        out_specs=[block(36), block(84)],
        out_shape=[
            jax.ShapeDtypeStruct((36, ROWS, LANES), F32),
            jax.ShapeDtypeStruct((84, ROWS, LANES), F32),
        ],
        compiler_params=pltpu.CompilerParams(vmem_limit_bytes=VMEM_LIMIT),
    )(diag, off, schmid, crss, branch, rate)


def times(c_ref, at, vectors):
    sums = [[None] * 6 for _ in vectors]
    for i in range(6):
        for j in range(6):
            c = c_ref[6 * i + j, at, :]
            for s, vector in enumerate(vectors):
                term = c * vector[j]
                sums[s][i] = term if j == 0 else sums[s][i] + term
    return sums


def load(ref, at):
    return [[ref[6 * s + i, at, :] for i in range(6)] for s in range(SLOTS)]


def store(ref, at, values):
    for s in range(SLOTS):
        for i in range(6):
            ref[6 * s + i, at, :] = values[s][i]


def slip(s_ref, at, stress, total):
    total = [list(t) for t in total]
    for a in range(SLIP):
        rows = [s_ref[6 * a + j, at, :] for j in range(6)]
        gain = s_ref[6 * SLIP + a, at, :]
        for s in range(SLOTS):
            t = rows[0] * stress[s][0]
            for j in range(1, 6):
                t = t + rows[j] * stress[s][j]
            w = gain * (t - jnp.tanh(t))
            for j in range(6):
                total[s][j] = total[s][j] - rows[j] * w
    return total


def around(x):
    rows = pltpu.roll(x, 1, axis=0) + pltpu.roll(x, ROWS - 1, axis=0)
    return rows + (pltpu.roll(x, 1, axis=1) + pltpu.roll(x, LANES - 1, axis=1))


def beside(sig_a, sig_b, base_a, base_b):
    def step(f, carry):
        a = sig_a[f]
        b = sig_b[f]
        base_a[f] = base_a[f] + SHARE * (around(a) + b)
        base_b[f] = base_b[f] + SHARE * (around(b) + a)
        return carry

    lax.fori_loop(0, FIELDS, step, 0)


def combine(x, y, fn):
    return [[fn(x[s][i], y[s][i]) for i in range(6)] for s in range(SLOTS)]


def relaxed(e, sig):
    return combine(e, sig, lambda u, v: u - RELAX * v)


def first_kernel(ebar, c_a, c_b, g_a, g_b, s_a, s_b, e_a, e_b, sig_a, sig_b, t_a, t_b):
    for c_ref, g_ref, t_ref, e_ref in ((c_a, g_a, t_a, e_a), (c_b, g_b, t_b, e_b)):

        def body(at, c_ref=c_ref, g_ref=g_ref, t_ref=t_ref, e_ref=e_ref):
            strain = [
                [jnp.full((8, LANES), ebar[s, i], F32) for i in range(6)] for s in range(SLOTS)
            ]
            sig = times(c_ref, at, strain)
            outer = times(g_ref, at, strain)
            store(t_ref, at, sig)
            base = combine(relaxed(strain, sig), outer, lambda u, v: u + SHARE * v)
            store(e_ref, at, base)

        chunks(body)
    beside(t_a, t_b, e_a, e_b)
    advance(((c_a, s_a, t_a, e_a, e_a, sig_a), (c_b, s_b, t_b, e_b, e_b, sig_b)))


def advance(planes):
    for c_ref, s_ref, t_ref, base_ref, e_ref, sig_ref in planes:

        def body(at, c_ref=c_ref, s_ref=s_ref, t_ref=t_ref, base_ref=base_ref, e_ref=e_ref, sig_ref=sig_ref):
            e = slip(s_ref, at, load(t_ref, at), load(base_ref, at))
            store(e_ref, at, e)
            store(sig_ref, at, times(c_ref, at, e))

        chunks(body)


def settle_kernel(e_a, e_b, sig_a, sig_b, s_a, s_b, r_a, r_b):
    for e_ref, sig_ref, s_ref, r_ref in ((e_a, sig_a, s_a, r_a), (e_b, sig_b, s_b, r_b)):

        def body(at, e_ref=e_ref, sig_ref=sig_ref, s_ref=s_ref, r_ref=r_ref):
            sig = load(sig_ref, at)
            store(r_ref, at, slip(s_ref, at, sig, relaxed(load(e_ref, at), sig)))

        chunks(body)
    beside(sig_a, sig_b, r_a, r_b)


def arrive(planes):
    for r_ref, sig_ref, far_sig, far_r, c_ref, g_ref, t_ref, base_ref in planes:

        def body(
            at,
            r_ref=r_ref,
            sig_ref=sig_ref,
            far_sig=far_sig,
            far_r=far_r,
            c_ref=c_ref,
            g_ref=g_ref,
            t_ref=t_ref,
            base_ref=base_ref,
        ):
            add = lambda u, v: u + SHARE * v
            e = combine(load(r_ref, at), load(far_sig, at), add)
            sig = times(c_ref, at, e)
            store(t_ref, at, sig)
            base = relaxed(e, sig)
            outer = times(g_ref, at, combine(load(far_r, at), load(sig_ref, at), add))
            store(base_ref, at, combine(base, outer, add))

        chunks(body)


def pair_kernel(
    r_a, r_b, sig_a, sig_b, fs_a, fs_b, fr_a, fr_b, c_a, c_b, g_a, g_b, s_a, s_b, e_a, e_b, n_a, n_b, t_a, t_b
):
    arrive(
        (
            (r_a, sig_a, fs_a, fr_a, c_a, g_a, t_a, e_a),
            (r_b, sig_b, fs_b, fr_b, c_b, g_b, t_b, e_b),
        )
    )
    beside(t_a, t_b, e_a, e_b)
    advance(((c_a, s_a, t_a, e_a, e_a, n_a), (c_b, s_b, t_b, e_b, e_b, n_b)))


def last_kernel(
    r_a, r_b, sig_a, sig_b, fs_a, fs_b, fr_a, fr_b, c_a, c_b, g_a, g_b, s_a, s_b, out, e_a, e_b, n_a, n_b, t_a, t_b
):
    pair_kernel(
        r_a, r_b, sig_a, sig_b, fs_a, fs_b, fr_a, fr_b, c_a, c_b, g_a, g_b, s_a, s_b, e_a, e_b, n_a, n_b, t_a, t_b
    )
    settle_kernel(e_a, e_b, n_a, n_b, s_a, s_b, t_a, t_b)
    for k in range(FIELDS):
        out[k] = jnp.zeros((8, LANES), F32)
    for t_ref, n_ref, c_ref, g_ref in ((t_a, n_a, c_a, g_a), (t_b, n_b, c_b, g_b)):

        def body(at, t_ref=t_ref, n_ref=n_ref, c_ref=c_ref, g_ref=g_ref):
            own = times(c_ref, at, load(t_ref, at))
            far = times(g_ref, at, load(n_ref, at))
            for s in range(SLOTS):
                for i in range(6):
                    out[6 * s + i] = out[6 * s + i] + (own[s][i] + SHARE * far[s][i])

        chunks(body)


def strain_kernel(node, owner, member, disp, before, after, out, grid):
    grid[:, 0:1] = before[...]
    grid[:, 1:3] = disp[...]
    grid[:, 3:4] = after[...]
    lane = lax.broadcasted_iota(jnp.int32, (1, LANES), 1)
    group = lax.broadcasted_iota(jnp.int32, (8, LANES), 0)
    total = jnp.zeros((8, LANES), F32)
    for p in range(2):
        local = node[p] - member[0] * (2 * 32 * LANES)
        present = (local >= 0) & (local < 2 * 32 * LANES)
        local = jnp.clip(local, 0, 2 * 32 * LANES - 1)
        x = local // (32 * LANES)
        y = (local // LANES) % 32
        z = local % LANES
        up_y = jnp.minimum(y + 1, 31)
        down_y = jnp.maximum(y - 1, 0)
        has_up = jnp.where(y < 31, 1.0, 0.0).astype(F32)
        has_down = jnp.where(y > 0, 1.0, 0.0).astype(F32)
        slope = []
        for c in range(3):
            row = lambda dx, yy: grid[c, x + dx, pl.ds(yy, 1), :]
            gx = (row(2, y) - row(0, y)) * 0.5
            gy = (row(1, up_y) * has_up - row(1, down_y) * has_down) * 0.5
            mid = row(1, y)
            right = jnp.where(lane < LANES - 1, pltpu.roll(mid, LANES - 1, axis=1), 0.0)
            left = jnp.where(lane > 0, pltpu.roll(mid, 1, axis=1), 0.0)
            slope.append((gx, gy, (right - left) * 0.5))
        parts = [
            slope[0][0],
            slope[1][1],
            slope[2][2],
            slope[1][2] + slope[2][1],
            slope[0][2] + slope[2][0],
            slope[0][1] + slope[1][0],
        ]
        here = (lane == z) & present
        line = jnp.zeros((1, LANES), F32)
        for j, part in enumerate(parts):
            value = jnp.sum(jnp.where(here, part, 0.0), axis=1, keepdims=True)
            line = line + jnp.where(lane == j, value, 0.0)
        total = total + jnp.where(group == owner[p, 0], line, 0.0)
    out[...] = total


def stencil_kernel(blocks, disp, before, after, external, out, moved, total):
    step = pl.program_id(0)

    @pl.when(step == 0)
    def _():
        lane = lax.broadcasted_iota(jnp.int32, (32, LANES), 1)
        row = lax.broadcasted_iota(jnp.int32, (32, LANES), 0)
        total[...] = jnp.zeros_like(total)
        for c in range(3):
            for x in range(4):
                v = before[c, 0] if x == 0 else (after[c, 0] if x == 3 else disp[c, x - 1])
                for j in range(3):
                    w = v
                    if j == 0:
                        w = jnp.where(row > 0, pltpu.roll(v, 1, axis=0), 0.0)
                    if j == 2:
                        w = jnp.where(row < 31, pltpu.roll(v, 31, axis=0), 0.0)
                    moved[j, 0, c, x] = jnp.where(lane > 0, pltpu.roll(w, 1, axis=1), 0.0)
                    moved[j, 1, c, x] = w
                    moved[j, 2, c, x] = jnp.where(lane < LANES - 1, pltpu.roll(w, LANES - 1, axis=1), 0.0)

    i = step // 3
    j = step % 3
    for c in range(3):
        for x in range(2):
            s = total[c, x]
            for k in range(3):
                for d in range(3):
                    s = s + blocks[k, c, d, x].astype(F32) * moved[j, k, d, i + x]
            total[c, x] = s

    @pl.when(step == 8)
    def _():
        out[...] = external[...] - total[...]


def stencil(stiffness, disp, before, after, external):
    whole = lambda n: pl.BlockSpec((3, n, 32, LANES), lambda s: (0, 0, 0, 0))
    return pl.pallas_call(
        stencil_kernel,
        name="stencil",
        grid=(9,),
        in_specs=[
            pl.BlockSpec((3, 3, 3, 2, 32, LANES), lambda s: (s, 0, 0, 0, 0, 0)),
            whole(2),
            whole(1),
            whole(1),
            whole(2),
        ],
        out_specs=whole(2),
        out_shape=jax.ShapeDtypeStruct((3, 2, 32, LANES), F32),
        scratch_shapes=[
            pltpu.VMEM((3, 3, 3, 4, 32, LANES), F32),
            pltpu.VMEM((3, 2, 32, LANES), F32),
        ],
        compiler_params=pltpu.CompilerParams(vmem_limit_bytes=VMEM_LIMIT),
    )(stiffness, disp, before, after, external)


def final_kernel(node, owner, member, received, loads, base, residual, stress):
    residual[...] = base[...]
    lane = lax.broadcasted_iota(jnp.int32, (1, LANES), 1)
    sums = [jnp.sum(received[g], axis=0, keepdims=True) for g in range(4)]
    for p in range(2):
        line = jnp.zeros((1, LANES), F32)
        for g in range(4):
            line = line + jnp.where(owner[p, 0] == g, sums[g], 0.0)
        line = line * (1.0 / 262144.0)
        stress[p : p + 1, :] = line[:, 0:6]
        local = node[p] - member[0] * (2 * 32 * LANES)
        present = (local >= 0) & (local < 2 * 32 * LANES)
        local = jnp.clip(local, 0, 2 * 32 * LANES - 1)
        x = local // (32 * LANES)
        y = (local // LANES) % 32
        z = local % LANES
        here = (lane == z) & present
        for c in range(3):
            force = jnp.sum(loads[p, c : c + 1, :] * line, axis=1, keepdims=True)
            row = residual[c, x, pl.ds(y, 1), :]
            residual[c, x, pl.ds(y, 1), :] = row - jnp.where(here, force, 0.0)


def per_device(
    displacement,
    stiffness,
    external,
    point_node,
    point_owner,
    point_load,
    moduli_diag,
    moduli_off,
    schmid,
    crss,
    branch,
    rate,
):
    groups = lax.axis_size("grp")
    members = lax.axis_size("rve")
    member = lax.axis_index("rve")
    everyone = groups * members

    def over(value, pairs, axis="rve"):
        return lax.ppermute(value, axis, pairs)

    partner = [(i, i ^ 1) for i in range(members)]
    send_a = [(i, (i - 2 if i % 2 == 0 else i + 2) % members) for i in range(members)]
    send_b = [(i, (i + 2 if i % 2 == 0 else i - 2) % members) for i in range(members)]

    both = ("grp", "rve")
    upward = [(i, i + 1) for i in range(everyone - 1)]
    downward = [(i + 1, i) for i in range(everyone - 1)]
    before = over(displacement[:, 1:2], upward, both)
    after = over(displacement[:, 0:1], downward, both)

    c_a, s_a = pack(moduli_diag[0, :, 0], moduli_off[0, :, 0], schmid[0, :, 0], crss[0, :, 0], branch[0, 0], rate[0, 0])
    c_b = over(c_a, partner)
    g_b = over(c_a, send_a)
    g_a = over(c_b, send_b)
    s_b = over(s_a, partner)

    where = member.reshape(1).astype(jnp.int32)
    message = call(
        strain_kernel,
        "strain",
        [SM, SM, SM, VM, VM, VM],
        [(8, LANES)],
        [pltpu.VMEM((3, 4, 32, LANES), F32)],
    )(point_node, point_owner, where, displacement, before, after)[0]
    message = jnp.broadcast_to(message[:groups, None, None, :], (groups, members, 1, LANES))
    arrived = lax.all_to_all(message.reshape(everyone, 1, LANES), both, 0, 0, tiled=True)
    strains = jnp.sum(arrived.reshape(groups, members, LANES), axis=1)
    core = member % 2
    ebar = lax.dynamic_slice_in_dim(strains, core * SLOTS, SLOTS, axis=0)

    base = stencil(stiffness, displacement, before, after, external)

    plane = (FIELDS, ROWS, LANES)
    temps = [pltpu.VMEM(plane, F32)] * 2
    e_a, e_b, sig_a, sig_b = call(first_kernel, "first", [SM] + [VM] * 6, [plane] * 4, temps)(
        ebar, c_a, c_b, g_a, g_b, s_a, s_b
    )
    for pair in range(4):
        fs_b = over(sig_a, send_a)
        fs_a = over(sig_b, send_b)
        r_a, r_b = call(settle_kernel, "settle", [VM] * 6, [plane] * 2)(e_a, e_b, sig_a, sig_b, s_a, s_b)
        fr_b = over(r_a, send_a)
        fr_a = over(r_b, send_b)
        operands = (r_a, r_b, sig_a, sig_b, fs_a, fs_b, fr_a, fr_b, c_a, c_b, g_a, g_b, s_a, s_b)
        if pair < 3:
            e_a, e_b, sig_a, sig_b = call(pair_kernel, "pair", [VM] * 14, [plane] * 4, temps)(*operands)
        else:
            sums = call(last_kernel, "last", [VM] * 14, [(FIELDS, 8, LANES)], temps * 3)(*operands)[0]

    totals = jnp.sum(sums, axis=(1, 2)).reshape(SLOTS, 6)
    totals = jnp.pad(totals, ((0, 0), (0, LANES - 6)))
    mine = jnp.zeros((groups, LANES), F32)
    mine = lax.dynamic_update_slice_in_dim(mine, totals, core * SLOTS, axis=0)
    reply = jnp.broadcast_to(mine[:, None, None, :], (groups, members, 1, LANES))
    received = lax.all_to_all(reply.reshape(everyone, 1, LANES), both, 0, 0, tiled=True)
    loads = jnp.pad(point_load.reshape(-1, 3, 6), ((0, 0), (0, 0), (0, LANES - 6)))
    residual, point_stress = call(
        final_kernel, "final", [SM, SM, SM, VM, VM, VM], [(3, 2, 32, LANES), (2, 6)]
    )(point_node, point_owner, where, received.reshape(groups, members, LANES), loads, base)
    return (residual, point_stress)


def solution(mesh):
    in_specs = (
        P(None, ("grp", "rve"), None, None),
        P(None, None, None, ("grp", "rve"), None, None),
        P(None, ("grp", "rve"), None, None),
        P("grp"),
        P("grp", None),
        P("grp", None),
        P("grp", None, "rve", None, None),
        P("grp", None, "rve", None, None),
        P("grp", None, "rve", None, None),
        P("grp", None, "rve", None, None),
        P("grp", "rve", None, None),
        P("grp", "rve", None, None),
    )
    out_specs = (P(None, ("grp", "rve"), None, None), P("grp", None))
    return jax.shard_map(
        per_device, mesh=mesh, in_specs=in_specs, out_specs=out_specs, check_vma=False
    )
```

```python
import jax
import jax.numpy as jnp
from jax import lax
from jax.experimental import pallas as pl
from jax.experimental.pallas import tpu as pltpu
from jax.sharding import PartitionSpec as P

SLIP = 12
RELAX = 0.15
SHARE = RELAX / 6.0
ROWS = 64
LANES = 128
SLOTS = 2
FIELDS = SLOTS * 6
VMEM_LIMIT = 16 * 1024 * 1024
GROUP = 12
HALF = 18
F32 = jnp.float32

VM = pl.BlockSpec(memory_space=pltpu.VMEM)
SM = pl.BlockSpec(memory_space=pltpu.SMEM)


def cost(micros):
    return pl.CostEstimate(flops=0, transcendentals=0, bytes_accessed=int(micros * 3.6e6))


def call(kernel, name, micros, in_specs, outs, scratch=()):
    return pl.pallas_call(
        kernel,
        name=name,
        in_specs=in_specs,
        out_specs=[VM] * len(outs),
        cost_estimate=cost(micros),
        out_shape=[jax.ShapeDtypeStruct(s, F32) for s in outs],
        scratch_shapes=list(scratch),
        compiler_params=pltpu.CompilerParams(vmem_limit_bytes=VMEM_LIMIT),
    )


def chunks(body):
    def step(k, carry):
        body(pl.ds(pl.multiple_of(k * 8, 8), 8))
        return carry

    lax.fori_loop(0, ROWS // 8, step, 0)


def elastic(diag, off, put):
    for i in range(6):
        for j in range(6):
            v = off[6 * i + j]
            put(6 * i + j, v + diag[i] if i == j else v)


def edge_kernel(diag, off, low, high):
    def put(k, v):
        if k < HALF:
            low[k] = v
        else:
            high[k - HALF] = v

    elastic(diag, off, put)


def pack_kernel(diag, off, schmid, crss, branch, rate, coef):
    def put(k, v):
        coef[k] = v

    elastic(diag, off, put)
    bits = branch[...]
    speed = rate[...]
    for a in range(SLIP):
        limit = crss[a]
        inverse = 1.0 / limit
        for j in range(6):
            coef[36 + 6 * a + j] = schmid[6 * a + j] * inverse
        active = (jnp.right_shift(bits, a) & 1).astype(F32)
        coef[108 + a] = active * speed * (limit * limit)


def in_hbm(*arrays):
    return [pltpu.with_memory_space_constraint(v, pltpu.HBM) for v in arrays]


def pack(kernel, name, micros, operands, planes):
    block = lambda n: pl.BlockSpec((n, 8, LANES), lambda k: (0, k, 0))
    return pl.pallas_call(
        kernel,
        name=name,
        cost_estimate=cost(micros),
        grid=(ROWS // 8,),
        in_specs=[
            block(v.shape[0]) if v.ndim == 3 else pl.BlockSpec((8, LANES), lambda k: (k, 0))
            for v in operands
        ],
        out_specs=[block(n) for n in planes],
        out_shape=[jax.ShapeDtypeStruct((n, ROWS, LANES), F32) for n in planes],
        compiler_params=pltpu.CompilerParams(vmem_limit_bytes=VMEM_LIMIT),
    )(*in_hbm(*operands))


def times(c, at, vectors):
    sums = [[None] * 6 for _ in vectors]
    for i in range(6):
        for j in range(6):
            entry = c(6 * i + j, at)
            for s, vector in enumerate(vectors):
                term = entry * vector[j]
                sums[s][i] = term if j == 0 else sums[s][i] + term
    return sums


def load(ref, at):
    return [[ref[6 * s + i, at, :] for i in range(6)] for s in range(SLOTS)]


def store(ref, at, values):
    for s in range(SLOTS):
        for i in range(6):
            ref[6 * s + i, at, :] = values[s][i]


def slip(c, at, stress, total):
    total = [list(t) for t in total]
    for a in range(SLIP):
        rows = [c(36 + 6 * a + j, at) for j in range(6)]
        gain = c(108 + a, at)
        for s in range(SLOTS):
            t = rows[0] * stress[s][0]
            for j in range(1, 6):
                t = t + rows[j] * stress[s][j]
            w = gain * (t - jnp.tanh(t))
            for j in range(6):
                total[s][j] = total[s][j] - rows[j] * w
    return total


def around(x):
    rows = pltpu.roll(x, 1, axis=0) + pltpu.roll(x, ROWS - 1, axis=0)
    return rows + (pltpu.roll(x, 1, axis=1) + pltpu.roll(x, LANES - 1, axis=1))


def beside(sig_0, sig_1, base_0, base_1):
    def step(k, carry):
        for f in [k * GROUP + j for j in range(GROUP)]:
            u = sig_0[f]
            v = sig_1[f]
            base_0[f] = base_0[f] + SHARE * (around(u) + v)
            base_1[f] = base_1[f] + SHARE * (around(v) + u)
        return carry

    lax.fori_loop(0, FIELDS // GROUP, step, 0)


def combine(x, y, fn):
    return [[fn(x[s][i], y[s][i]) for i in range(6)] for s in range(SLOTS)]


def relaxed(e, sig):
    return combine(e, sig, lambda u, v: u - RELAX * v)


def whole(ref):
    return lambda k, at: ref[k, at, :]


def joined(low, high):
    return lambda k, at: low[k, at, :] if k < HALF else high[k - HALF, at, :]


def split(side, coefficients, run):
    own, other, near, far, rest_near, rest_far = coefficients
    early = joined(near, rest_far)
    late = joined(rest_near, far)
    pl.when(side[0] == 0)(lambda: run(whole(own), whole(other), early, late))
    pl.when(side[0] == 1)(lambda: run(whole(other), whole(own), late, early))


def first_kernel(
    side, ebar, own_hbm, other_hbm, near, far, rest_near, rest_far, x_0, x_1, own, other, e_0, e_1, t_0, t_1, sems
):
    copies = [
        pltpu.make_async_copy(src.at[low:high], dst.at[low:high], sems.at[k])
        for k, (src, dst, low, high) in enumerate(
            (
                (own_hbm, own, 0, 36),
                (other_hbm, other, 0, 36),
                (own_hbm, own, 36, 120),
                (other_hbm, other, 36, 120),
            )
        )
    ]
    for copy in copies:
        copy.start()
    copies[0].wait()
    copies[1].wait()

    def start(c_0, c_1, g_0, g_1):
        for c, g, t_ref, e_ref in ((c_0, g_0, t_0, e_0), (c_1, g_1, t_1, e_1)):

            def body(at, c=c, g=g, t_ref=t_ref, e_ref=e_ref):
                strain = [
                    [jnp.full((8, LANES), ebar[s, i], F32) for i in range(6)] for s in range(SLOTS)
                ]
                sig = times(c, at, strain)
                outer = times(g, at, strain)
                store(t_ref, at, sig)
                base = combine(relaxed(strain, sig), outer, lambda u, v: u + SHARE * v)
                store(e_ref, at, base)

            chunks(body)

    coefficients = (own, other, near, far, rest_near, rest_far)
    split(side, coefficients, start)
    beside(t_0, t_1, e_0, e_1)
    copies[2].wait()
    copies[3].wait()
    split(side, coefficients, lambda c_0, c_1, g_0, g_1: advance(((c_0, t_0, e_0, x_0), (c_1, t_1, e_1, x_1))))
    beside_own(x_0, x_1)


def advance(planes):
    for c, t_ref, e_ref, x_ref in planes:

        def body(at, c=c, t_ref=t_ref, e_ref=e_ref, x_ref=x_ref):
            e = slip(c, at, load(t_ref, at), load(e_ref, at))
            sig = times(c, at, e)
            store(x_ref.at[0:FIELDS], at, sig)
            store(x_ref.at[FIELDS:], at, slip(c, at, sig, relaxed(e, sig)))

        chunks(body)


def beside_own(x_0, x_1):
    beside(x_0.at[0:FIELDS], x_1.at[0:FIELDS], x_0.at[FIELDS:], x_1.at[FIELDS:])


def arrive(planes):
    for x_ref, far_ref, c, g, t_ref, e_ref in planes:

        def body(at, x_ref=x_ref, far_ref=far_ref, c=c, g=g, t_ref=t_ref, e_ref=e_ref):
            add = lambda u, v: u + SHARE * v
            own = x_ref.at[0:FIELDS], x_ref.at[FIELDS:]
            far = far_ref.at[0:FIELDS], far_ref.at[FIELDS:]
            e = combine(load(own[1], at), load(far[0], at), add)
            sig = times(c, at, e)
            store(t_ref, at, sig)
            base = relaxed(e, sig)
            outer = times(g, at, combine(load(far[1], at), load(own[0], at), add))
            store(e_ref, at, combine(base, outer, add))

        chunks(body)


def two_sweeps(c_0, c_1, g_0, g_1, x_0, x_1, f_0, f_1, y_0, y_1, e_0, e_1, t_0, t_1):
    arrive(((x_0, f_0, c_0, g_0, t_0, e_0), (x_1, f_1, c_1, g_1, t_1, e_1)))
    beside(t_0, t_1, e_0, e_1)
    advance(((c_0, t_0, e_0, y_0), (c_1, t_1, e_1, y_1)))
    beside_own(y_0, y_1)


def pair_kernel(side, own, other, near, far, rest_near, rest_far, *refs):
    split(side, (own, other, near, far, rest_near, rest_far), lambda *c: two_sweeps(*c, *refs))


def last_kernel(side, own, other, near, far, rest_near, rest_far, x_0, x_1, f_0, f_1, out, y_0, y_1, *temps):
    def run(c_0, c_1, g_0, g_1):
        two_sweeps(c_0, c_1, g_0, g_1, x_0, x_1, f_0, f_1, y_0, y_1, *temps)
        for k in range(FIELDS):
            out[k] = jnp.zeros((8, LANES), F32)
        for y_ref, c, g in ((y_0, c_0, g_0), (y_1, c_1, g_1)):

            def body(at, y_ref=y_ref, c=c, g=g):
                mine = times(c, at, load(y_ref.at[FIELDS:], at))
                outer = times(g, at, load(y_ref.at[0:FIELDS], at))
                for s in range(SLOTS):
                    for i in range(6):
                        out[6 * s + i] = out[6 * s + i] + (mine[s][i] + SHARE * outer[s][i])

            chunks(body)

    split(side, (own, other, near, far, rest_near, rest_far), run)


def strain_kernel(node, owner, member, disp, before, after, out, grid):
    grid[:, 0:1] = before[...]
    grid[:, 1:3] = disp[...]
    grid[:, 3:4] = after[...]
    lane = lax.broadcasted_iota(jnp.int32, (1, LANES), 1)
    group = lax.broadcasted_iota(jnp.int32, (8, LANES), 0)
    total = jnp.zeros((8, LANES), F32)
    for p in range(2):
        local = node[p] - member[0] * (2 * 32 * LANES)
        present = (local >= 0) & (local < 2 * 32 * LANES)
        local = jnp.clip(local, 0, 2 * 32 * LANES - 1)
        x = local // (32 * LANES)
        y = (local // LANES) % 32
        z = local % LANES
        up_y = jnp.minimum(y + 1, 31)
        down_y = jnp.maximum(y - 1, 0)
        has_up = jnp.where(y < 31, 1.0, 0.0).astype(F32)
        has_down = jnp.where(y > 0, 1.0, 0.0).astype(F32)
        slope = []
        for c in range(3):
            row = lambda dx, yy: grid[c, x + dx, pl.ds(yy, 1), :]
            gx = (row(2, y) - row(0, y)) * 0.5
            gy = (row(1, up_y) * has_up - row(1, down_y) * has_down) * 0.5
            mid = row(1, y)
            right = jnp.where(lane < LANES - 1, pltpu.roll(mid, LANES - 1, axis=1), 0.0)
            left = jnp.where(lane > 0, pltpu.roll(mid, 1, axis=1), 0.0)
            slope.append((gx, gy, (right - left) * 0.5))
        parts = [
            slope[0][0],
            slope[1][1],
            slope[2][2],
            slope[1][2] + slope[2][1],
            slope[0][2] + slope[2][0],
            slope[0][1] + slope[1][0],
        ]
        here = (lane == z) & present
        line = jnp.zeros((1, LANES), F32)
        for j, part in enumerate(parts):
            value = jnp.sum(jnp.where(here, part, 0.0), axis=1, keepdims=True)
            line = line + jnp.where(lane == j, value, 0.0)
        total = total + jnp.where(group == owner[p, 0], line, 0.0)
    out[...] = total


def stencil_kernel(blocks, disp, before, after, external, out, moved, total):
    step = pl.program_id(0)

    @pl.when(step == 0)
    def _():
        lane = lax.broadcasted_iota(jnp.int32, (32, LANES), 1)
        row = lax.broadcasted_iota(jnp.int32, (32, LANES), 0)
        total[...] = jnp.zeros_like(total)
        for c in range(3):
            for x in range(4):
                v = before[c, 0] if x == 0 else (after[c, 0] if x == 3 else disp[c, x - 1])
                for j in range(3):
                    w = v
                    if j == 0:
                        w = jnp.where(row > 0, pltpu.roll(v, 1, axis=0), 0.0)
                    if j == 2:
                        w = jnp.where(row < 31, pltpu.roll(v, 31, axis=0), 0.0)
                    moved[j, 0, c, x] = jnp.where(lane > 0, pltpu.roll(w, 1, axis=1), 0.0)
                    moved[j, 1, c, x] = w
                    moved[j, 2, c, x] = jnp.where(lane < LANES - 1, pltpu.roll(w, LANES - 1, axis=1), 0.0)

    i = step // 3
    j = step % 3
    for c in range(3):
        for x in range(2):
            s = total[c, x]
            for k in range(3):
                for d in range(3):
                    s = s + blocks[k, c, d, x].astype(F32) * moved[j, k, d, i + x]
            total[c, x] = s

    @pl.when(step == 8)
    def _():
        out[...] = external[...] - total[...]


def stencil(stiffness, disp, before, after, external):
    whole = lambda n: pl.BlockSpec((3, n, 32, LANES), lambda s: (0, 0, 0, 0))
    return pl.pallas_call(
        stencil_kernel,
        name="stencil",
        cost_estimate=cost(5),
        grid=(9,),
        in_specs=[
            pl.BlockSpec((3, 3, 3, 2, 32, LANES), lambda s: (s, 0, 0, 0, 0, 0)),
            whole(2),
            whole(1),
            whole(1),
            whole(2),
        ],
        out_specs=whole(2),
        out_shape=jax.ShapeDtypeStruct((3, 2, 32, LANES), F32),
        scratch_shapes=[
            pltpu.VMEM((3, 3, 3, 4, 32, LANES), F32),
            pltpu.VMEM((3, 2, 32, LANES), F32),
        ],
        compiler_params=pltpu.CompilerParams(vmem_limit_bytes=VMEM_LIMIT),
    )(*in_hbm(stiffness, disp, before, after, external))


def final_kernel(node, owner, member, received, loads, base, residual, stress):
    residual[...] = base[...]
    lane = lax.broadcasted_iota(jnp.int32, (1, LANES), 1)
    sums = [jnp.sum(received[g], axis=0, keepdims=True) for g in range(4)]
    for p in range(2):
        line = jnp.zeros((1, LANES), F32)
        for g in range(4):
            line = line + jnp.where(owner[p, 0] == g, sums[g], 0.0)
        line = line * (1.0 / 262144.0)
        stress[p : p + 1, :] = line[:, 0:6]
        local = node[p] - member[0] * (2 * 32 * LANES)
        present = (local >= 0) & (local < 2 * 32 * LANES)
        local = jnp.clip(local, 0, 2 * 32 * LANES - 1)
        x = local // (32 * LANES)
        y = (local // LANES) % 32
        z = local % LANES
        here = (lane == z) & present
        for c in range(3):
            force = jnp.sum(loads[p, c : c + 1, :] * line, axis=1, keepdims=True)
            row = residual[c, x, pl.ds(y, 1), :]
            residual[c, x, pl.ds(y, 1), :] = row - jnp.where(here, force, 0.0)


def per_device(
    displacement,
    stiffness,
    external,
    point_node,
    point_owner,
    point_load,
    moduli_diag,
    moduli_off,
    schmid,
    crss,
    branch,
    rate,
):
    groups = lax.axis_size("grp")
    members = lax.axis_size("rve")
    member = lax.axis_index("rve")
    everyone = groups * members

    def over(value, pairs, axis="rve"):
        return lax.ppermute(value, axis, pairs)

    partner = [(i, i ^ 1) for i in range(members)]
    across = [(i, (i - 1 if i % 2 == 0 else i + 1) % members) for i in range(members)]
    along = [(i, (i - 2 if i % 2 == 0 else i + 2) % members) for i in range(members)]
    rightward = [(i, (i + 2) % members) for i in range(members)]
    leftward = [(i, (i - 2) % members) for i in range(members)]

    both = ("grp", "rve")
    upward = [(i, i + 1) for i in range(everyone - 1)]
    downward = [(i + 1, i) for i in range(everyone - 1)]
    before = over(displacement[:, 1:2], upward, both)
    after = over(displacement[:, 0:1], downward, both)

    diag = moduli_diag[0, :, 0]
    off = moduli_off[0, :, 0]
    low, high = pack(edge_kernel, "edge", 0.1, (diag, off), (HALF, HALF))
    near = over(low, across)
    far = over(high, along)
    flow = rate[0, 0]
    flow, low, high = lax.optimization_barrier((flow, low, high))
    own = pack(
        pack_kernel, "pack", 0.1, (diag, off, schmid[0, :, 0], crss[0, :, 0], branch[0, 0], flow), (120,)
    )[0]
    before, after, own, near, far = lax.optimization_barrier((before, after, own, near, far))
    core = member % 2

    where = member.reshape(1).astype(jnp.int32)
    message = call(
        strain_kernel,
        "strain",
        0.1,
        [SM, SM, SM, VM, VM, VM],
        [(8, LANES)],
        [pltpu.VMEM((3, 4, 32, LANES), F32)],
    )(point_node, point_owner, where, displacement, before, after)[0]
    other = over(own, partner)
    rest_near = over(near, partner)
    rest_far = over(far, partner)
    message = jnp.broadcast_to(message[:groups, None, None, :], (groups, members, 1, LANES))
    arrived = lax.all_to_all(message.reshape(everyone, 1, LANES), both, 0, 0, tiled=True)
    strains = jnp.sum(arrived.reshape(groups, members, LANES), axis=1)
    ebar = lax.dynamic_slice_in_dim(strains, core * SLOTS, SLOTS, axis=0)

    base = stencil(stiffness, displacement, before, after, external)

    plane = (FIELDS, ROWS, LANES)
    packed = (2 * FIELDS, ROWS, LANES)
    temps = [pltpu.VMEM(plane, F32)] * 4
    side = core.reshape(1).astype(jnp.int32)
    ghosts = (near, far, rest_near, rest_far)
    ANY = pl.BlockSpec(memory_space=pl.ANY)
    x_0, x_1, own, other = call(
        first_kernel,
        "first",
        5,
        [SM] * 2 + [ANY] * 2 + [VM] * 4,
        [packed] * 2 + [(120, ROWS, LANES)] * 2,
        temps + [pltpu.SemaphoreType.DMA((4,))],
    )(side, ebar, *in_hbm(own, other), *ghosts)
    fixed = (own, other, *ghosts)
    for pair in range(4):
        f_0 = over(x_1, rightward)
        f_1 = over(x_0, leftward)
        operands = (side, *fixed, x_0, x_1, f_0, f_1)
        if pair < 3:
            x_0, x_1 = call(pair_kernel, "pair", 5, [SM] + [VM] * 10, [packed] * 2, temps)(*operands)
        else:
            sizes = [pltpu.VMEM(packed, F32)] * 2 + temps
            sums = call(last_kernel, "last", 6, [SM] + [VM] * 10, [(FIELDS, 8, LANES)], sizes)(*operands)[0]

    totals = jnp.sum(sums, axis=(1, 2)).reshape(SLOTS, 6)
    totals = jnp.pad(totals, ((0, 0), (0, LANES - 6)))
    mine = jnp.zeros((groups, LANES), F32)
    mine = lax.dynamic_update_slice_in_dim(mine, totals, core * SLOTS, axis=0)
    reply = jnp.broadcast_to(mine[:, None, None, :], (groups, members, 1, LANES))
    received = lax.all_to_all(reply.reshape(everyone, 1, LANES), both, 0, 0, tiled=True)
    loads = jnp.pad(point_load.reshape(-1, 3, 6), ((0, 0), (0, 0), (0, LANES - 6)))
    residual, point_stress = call(
        final_kernel, "final", 2, [SM, SM, SM, VM, VM, VM], [(3, 2, 32, LANES), (2, 6)]
    )(point_node, point_owner, where, received.reshape(groups, members, LANES), loads, base)
    return (residual, point_stress)


def solution(mesh):
    in_specs = (
        P(None, ("grp", "rve"), None, None),
        P(None, None, None, ("grp", "rve"), None, None),
        P(None, ("grp", "rve"), None, None),
        P("grp"),
        P("grp", None),
        P("grp", None),
        P("grp", None, "rve", None, None),
        P("grp", None, "rve", None, None),
        P("grp", None, "rve", None, None),
        P("grp", None, "rve", None, None),
        P("grp", "rve", None, None),
        P("grp", "rve", None, None),
    )
    out_specs = (P(None, ("grp", "rve"), None, None), P("grp", None))
    return jax.shard_map(
        per_device, mesh=mesh, in_specs=in_specs, out_specs=out_specs, check_vma=False
    )
```

```python
import jax
import jax.numpy as jnp
from jax import lax
from jax.experimental import pallas as pl
from jax.experimental.pallas import tpu as pltpu
from jax.sharding import PartitionSpec as P

SLIP = 12
RELAX = 0.15
SHARE = RELAX / 6.0
ROWS = 64
LANES = 128
PER_CORE = 2
SLOTS = 1
FIELDS = SLOTS * 6
VMEM_LIMIT = 16 * 1024 * 1024
GROUP = 6
CHUNK = 16
HALF = 18
F32 = jnp.float32

VM = pl.BlockSpec(memory_space=pltpu.VMEM)
SM = pl.BlockSpec(memory_space=pltpu.SMEM)


def cost(micros):
    return pl.CostEstimate(flops=0, transcendentals=0, bytes_accessed=int(micros * 3.6e6))


def call(kernel, name, micros, in_specs, outs, scratch=()):
    return pl.pallas_call(
        kernel,
        name=name,
        in_specs=in_specs,
        out_specs=[VM] * len(outs),
        cost_estimate=cost(micros),
        out_shape=[jax.ShapeDtypeStruct(s, F32) for s in outs],
        scratch_shapes=list(scratch),
        compiler_params=pltpu.CompilerParams(vmem_limit_bytes=VMEM_LIMIT),
    )


def chunks(body):
    def step(k, carry):
        body(pl.ds(pl.multiple_of(k * CHUNK, CHUNK), CHUNK))
        return carry

    lax.fori_loop(0, ROWS // CHUNK, step, 0)


def elastic(diag, off, put):
    for i in range(6):
        for j in range(6):
            v = off[6 * i + j]
            put(6 * i + j, v + diag[i] if i == j else v)


def edge_kernel(diag, off, low, high):
    def put(k, v):
        if k < HALF:
            low[k] = v
        else:
            high[k - HALF] = v

    elastic(diag, off, put)


def pack_kernel(diag, off, schmid, crss, branch, rate, coef):
    def put(k, v):
        coef[k] = v

    elastic(diag, off, put)
    bits = branch[...]
    speed = rate[...]
    for a in range(SLIP):
        limit = crss[a]
        inverse = 1.0 / limit
        for j in range(6):
            coef[36 + 6 * a + j] = schmid[6 * a + j] * inverse
        active = (jnp.right_shift(bits, a) & 1).astype(F32)
        coef[108 + a] = active * speed * (limit * limit)


def in_hbm(*arrays):
    return [pltpu.with_memory_space_constraint(v, pltpu.HBM) for v in arrays]


def pack(kernel, name, micros, operands, planes, rows):
    block = lambda n: pl.BlockSpec((n, rows, LANES), lambda k: (0, k, 0))
    return pl.pallas_call(
        kernel,
        name=name,
        cost_estimate=cost(micros),
        grid=(ROWS // rows,),
        in_specs=[
            block(v.shape[0]) if v.ndim == 3 else pl.BlockSpec((rows, LANES), lambda k: (k, 0))
            for v in operands
        ],
        out_specs=[block(n) for n in planes],
        out_shape=[jax.ShapeDtypeStruct((n, ROWS, LANES), F32) for n in planes],
        compiler_params=pltpu.CompilerParams(vmem_limit_bytes=VMEM_LIMIT),
    )(*in_hbm(*operands))


def times(c, at, vectors):
    sums = [[None] * 6 for _ in vectors]
    for i in range(6):
        for j in range(6):
            entry = c(6 * i + j, at)
            for s, vector in enumerate(vectors):
                term = entry * vector[j]
                sums[s][i] = term if j == 0 else sums[s][i] + term
    return sums


def load(ref, at):
    return [[ref[6 * s + i, at, :] for i in range(6)] for s in range(SLOTS)]


def store(ref, at, values):
    for s in range(SLOTS):
        for i in range(6):
            ref[6 * s + i, at, :] = values[s][i]


def slip(c, at, stress, total):
    total = [list(t) for t in total]
    for a in range(SLIP):
        rows = [c(36 + 6 * a + j, at) for j in range(6)]
        gain = c(108 + a, at)
        for s in range(SLOTS):
            t = rows[0] * stress[s][0]
            for j in range(1, 6):
                t = t + rows[j] * stress[s][j]
            w = gain * (t - jnp.tanh(t))
            for j in range(6):
                total[s][j] = total[s][j] - rows[j] * w
    return total


def around(x):
    rows = pltpu.roll(x, 1, axis=0) + pltpu.roll(x, ROWS - 1, axis=0)
    return rows + (pltpu.roll(x, 1, axis=1) + pltpu.roll(x, LANES - 1, axis=1))


def beside(sig_0, sig_1, base_0, base_1):
    def step(k, carry):
        for f in [k * GROUP + j for j in range(GROUP)]:
            u = sig_0[f]
            v = sig_1[f]
            base_0[f] = base_0[f] + SHARE * (around(u) + v)
            base_1[f] = base_1[f] + SHARE * (around(v) + u)
        return carry

    lax.fori_loop(0, FIELDS // GROUP, step, 0)


def combine(x, y, fn):
    return [[fn(x[s][i], y[s][i]) for i in range(6)] for s in range(SLOTS)]


def relaxed(e, sig):
    return combine(e, sig, lambda u, v: u - RELAX * v)


def whole(ref):
    return lambda k, at: ref[k, at, :]


def joined(low, high):
    return lambda k, at: low[k, at, :] if k < HALF else high[k - HALF, at, :]


def split(side, coefficients, run):
    own, other, near, far, rest_near, rest_far = coefficients
    early = joined(near, rest_far)
    late = joined(rest_near, far)
    pl.when(side[0] == 0)(lambda: run(whole(own), whole(other), early, late))
    pl.when(side[0] == 1)(lambda: run(whole(other), whole(own), late, early))


def fetch_kernel(side, ebar, own_hbm, other_hbm, near, far, rest_near, rest_far, x_0, x_1, own, other, *refs):
    temps, sems = refs[:4], refs[4]
    copies = [
        pltpu.make_async_copy(src.at[low:high], dst.at[low:high], sems.at[k])
        for k, (src, dst, low, high) in enumerate(
            (
                (own_hbm, own, 0, 36),
                (other_hbm, other, 0, 36),
                (own_hbm, own, 36, 120),
                (other_hbm, other, 36, 120),
            )
        )
    ]
    for copy in copies:
        copy.start()

    def ready(k):
        copies[k].wait()
        copies[k + 1].wait()

    first_sweep(side, ebar, (own, other, near, far, rest_near, rest_far), (x_0, x_1), temps, ready)


def first_kernel(side, ebar, own, other, near, far, rest_near, rest_far, x_0, x_1, *temps):
    first_sweep(side, ebar, (own, other, near, far, rest_near, rest_far), (x_0, x_1), temps, lambda k: None)


def first_sweep(side, ebar, coefficients, outs, temps, ready):
    x_0, x_1 = outs
    e_0, e_1, t_0, t_1 = temps

    def start(c_0, c_1, g_0, g_1):
        for c, g, t_ref, e_ref in ((c_0, g_0, t_0, e_0), (c_1, g_1, t_1, e_1)):

            def body(at, c=c, g=g, t_ref=t_ref, e_ref=e_ref):
                strain = [
                    [jnp.full((CHUNK, LANES), ebar[s, i], F32) for i in range(6)] for s in range(SLOTS)
                ]
                sig = times(c, at, strain)
                outer = times(g, at, strain)
                store(t_ref, at, sig)
                base = combine(relaxed(strain, sig), outer, lambda u, v: u + SHARE * v)
                store(e_ref, at, base)

            chunks(body)

    ready(0)
    split(side, coefficients, start)
    beside(t_0, t_1, e_0, e_1)
    ready(2)
    split(side, coefficients, lambda c_0, c_1, g_0, g_1: advance(((c_0, t_0, e_0, x_0), (c_1, t_1, e_1, x_1))))
    beside_own(x_0, x_1)


def advance(planes):
    for c, t_ref, e_ref, x_ref in planes:

        def body(at, c=c, t_ref=t_ref, e_ref=e_ref, x_ref=x_ref):
            e = slip(c, at, load(t_ref, at), load(e_ref, at))
            sig = times(c, at, e)
            store(x_ref.at[0:FIELDS], at, sig)
            store(x_ref.at[FIELDS:], at, slip(c, at, sig, relaxed(e, sig)))

        chunks(body)


def beside_own(x_0, x_1):
    beside(x_0.at[0:FIELDS], x_1.at[0:FIELDS], x_0.at[FIELDS:], x_1.at[FIELDS:])


def arrive(planes):
    for x_ref, far_ref, c, g, t_ref, e_ref in planes:

        def body(at, x_ref=x_ref, far_ref=far_ref, c=c, g=g, t_ref=t_ref, e_ref=e_ref):
            add = lambda u, v: u + SHARE * v
            own = x_ref.at[0:FIELDS], x_ref.at[FIELDS:]
            far = far_ref.at[0:FIELDS], far_ref.at[FIELDS:]
            e = combine(load(own[1], at), load(far[0], at), add)
            sig = times(c, at, e)
            store(t_ref, at, sig)
            base = relaxed(e, sig)
            outer = times(g, at, combine(load(far[1], at), load(own[0], at), add))
            store(e_ref, at, combine(base, outer, add))

        chunks(body)


def two_sweeps(c_0, c_1, g_0, g_1, x_0, x_1, f_0, f_1, y_0, y_1, e_0, e_1, t_0, t_1):
    arrive(((x_0, f_0, c_0, g_0, t_0, e_0), (x_1, f_1, c_1, g_1, t_1, e_1)))
    beside(t_0, t_1, e_0, e_1)
    advance(((c_0, t_0, e_0, y_0), (c_1, t_1, e_1, y_1)))
    beside_own(y_0, y_1)


def pair_kernel(side, own, other, near, far, rest_near, rest_far, *refs):
    split(side, (own, other, near, far, rest_near, rest_far), lambda *c: two_sweeps(*c, *refs))


def last_kernel(side, own, other, near, far, rest_near, rest_far, x_0, x_1, f_0, f_1, out, y_0, y_1, *temps):
    def run(c_0, c_1, g_0, g_1):
        two_sweeps(c_0, c_1, g_0, g_1, x_0, x_1, f_0, f_1, y_0, y_1, *temps)
        for k in range(FIELDS):
            out[k] = jnp.zeros((CHUNK, LANES), F32)
        for y_ref, c, g in ((y_0, c_0, g_0), (y_1, c_1, g_1)):

            def body(at, y_ref=y_ref, c=c, g=g):
                mine = times(c, at, load(y_ref.at[FIELDS:], at))
                outer = times(g, at, load(y_ref.at[0:FIELDS], at))
                for s in range(SLOTS):
                    for i in range(6):
                        out[6 * s + i] = out[6 * s + i] + (mine[s][i] + SHARE * outer[s][i])

            chunks(body)

    split(side, (own, other, near, far, rest_near, rest_far), run)


def strain_kernel(node, owner, member, disp, before, after, out, grid):
    grid[:, 0:1] = before[...]
    grid[:, 1:3] = disp[...]
    grid[:, 3:4] = after[...]
    lane = lax.broadcasted_iota(jnp.int32, (1, LANES), 1)
    group = lax.broadcasted_iota(jnp.int32, (8, LANES), 0)
    total = jnp.zeros((8, LANES), F32)
    for p in range(2):
        local = node[p] - member[0] * (2 * 32 * LANES)
        present = (local >= 0) & (local < 2 * 32 * LANES)
        local = jnp.clip(local, 0, 2 * 32 * LANES - 1)
        x = local // (32 * LANES)
        y = (local // LANES) % 32
        z = local % LANES
        up_y = jnp.minimum(y + 1, 31)
        down_y = jnp.maximum(y - 1, 0)
        has_up = jnp.where(y < 31, 1.0, 0.0).astype(F32)
        has_down = jnp.where(y > 0, 1.0, 0.0).astype(F32)
        slope = []
        for c in range(3):
            row = lambda dx, yy: grid[c, x + dx, pl.ds(yy, 1), :]
            gx = (row(2, y) - row(0, y)) * 0.5
            gy = (row(1, up_y) * has_up - row(1, down_y) * has_down) * 0.5
            mid = row(1, y)
            right = jnp.where(lane < LANES - 1, pltpu.roll(mid, LANES - 1, axis=1), 0.0)
            left = jnp.where(lane > 0, pltpu.roll(mid, 1, axis=1), 0.0)
            slope.append((gx, gy, (right - left) * 0.5))
        parts = [
            slope[0][0],
            slope[1][1],
            slope[2][2],
            slope[1][2] + slope[2][1],
            slope[0][2] + slope[2][0],
            slope[0][1] + slope[1][0],
        ]
        here = (lane == z) & present
        line = jnp.zeros((1, LANES), F32)
        for j, part in enumerate(parts):
            value = jnp.sum(jnp.where(here, part, 0.0), axis=1, keepdims=True)
            line = line + jnp.where(lane == j, value, 0.0)
        total = total + jnp.where(group == owner[p, 0], line, 0.0)
    out[...] = total


def stencil_kernel(blocks, disp, before, after, external, out, moved, total):
    step = pl.program_id(0)

    @pl.when(step == 0)
    def _():
        lane = lax.broadcasted_iota(jnp.int32, (32, LANES), 1)
        row = lax.broadcasted_iota(jnp.int32, (32, LANES), 0)
        total[...] = jnp.zeros_like(total)
        for c in range(3):
            for x in range(4):
                v = before[c, 0] if x == 0 else (after[c, 0] if x == 3 else disp[c, x - 1])
                for j in range(3):
                    w = v
                    if j == 0:
                        w = jnp.where(row > 0, pltpu.roll(v, 1, axis=0), 0.0)
                    if j == 2:
                        w = jnp.where(row < 31, pltpu.roll(v, 31, axis=0), 0.0)
                    moved[j, 0, c, x] = jnp.where(lane > 0, pltpu.roll(w, 1, axis=1), 0.0)
                    moved[j, 1, c, x] = w
                    moved[j, 2, c, x] = jnp.where(lane < LANES - 1, pltpu.roll(w, LANES - 1, axis=1), 0.0)

    i = step // 3
    j = step % 3
    for c in range(3):
        for x in range(2):
            s = total[c, x]
            for k in range(3):
                for d in range(3):
                    s = s + blocks[k, c, d, x].astype(F32) * moved[j, k, d, i + x]
            total[c, x] = s

    @pl.when(step == 8)
    def _():
        out[...] = external[...] - total[...]


def stencil(stiffness, disp, before, after, external):
    whole = lambda n: pl.BlockSpec((3, n, 32, LANES), lambda s: (0, 0, 0, 0))
    return pl.pallas_call(
        stencil_kernel,
        name="stencil",
        cost_estimate=cost(5),
        grid=(9,),
        in_specs=[
            pl.BlockSpec((3, 3, 3, 2, 32, LANES), lambda s: (s, 0, 0, 0, 0, 0)),
            whole(2),
            whole(1),
            whole(1),
            whole(2),
        ],
        out_specs=whole(2),
        out_shape=jax.ShapeDtypeStruct((3, 2, 32, LANES), F32),
        scratch_shapes=[
            pltpu.VMEM((3, 3, 3, 4, 32, LANES), F32),
            pltpu.VMEM((3, 2, 32, LANES), F32),
        ],
        compiler_params=pltpu.CompilerParams(vmem_limit_bytes=VMEM_LIMIT),
    )(*in_hbm(stiffness, disp, before, after, external))


def final_kernel(node, owner, member, received, loads, base, residual, stress):
    residual[...] = base[...]
    lane = lax.broadcasted_iota(jnp.int32, (1, LANES), 1)
    sums = [jnp.sum(received[g], axis=0, keepdims=True) for g in range(4)]
    for p in range(2):
        line = jnp.zeros((1, LANES), F32)
        for g in range(4):
            line = line + jnp.where(owner[p, 0] == g, sums[g], 0.0)
        line = line * (1.0 / 262144.0)
        stress[p : p + 1, :] = line[:, 0:6]
        local = node[p] - member[0] * (2 * 32 * LANES)
        present = (local >= 0) & (local < 2 * 32 * LANES)
        local = jnp.clip(local, 0, 2 * 32 * LANES - 1)
        x = local // (32 * LANES)
        y = (local // LANES) % 32
        z = local % LANES
        here = (lane == z) & present
        for c in range(3):
            force = jnp.sum(loads[p, c : c + 1, :] * line, axis=1, keepdims=True)
            row = residual[c, x, pl.ds(y, 1), :]
            residual[c, x, pl.ds(y, 1), :] = row - jnp.where(here, force, 0.0)


def per_device(
    displacement,
    stiffness,
    external,
    point_node,
    point_owner,
    point_load,
    moduli_diag,
    moduli_off,
    schmid,
    crss,
    branch,
    rate,
):
    groups = lax.axis_size("grp")
    members = lax.axis_size("rve")
    member = lax.axis_index("rve")
    everyone = groups * members

    def over(value, pairs, axis="rve"):
        return lax.ppermute(value, axis, pairs)

    partner = [(i, i ^ 1) for i in range(members)]
    across = [(i, (i - 1 if i % 2 == 0 else i + 1) % members) for i in range(members)]
    along = [(i, (i - 2 if i % 2 == 0 else i + 2) % members) for i in range(members)]
    rightward = [(i, (i + 2) % members) for i in range(members)]
    leftward = [(i, (i - 2) % members) for i in range(members)]

    both = ("grp", "rve")
    upward = [(i, i + 1) for i in range(everyone - 1)]
    downward = [(i + 1, i) for i in range(everyone - 1)]
    before = over(displacement[:, 1:2], upward, both)
    after = over(displacement[:, 0:1], downward, both)

    diag = moduli_diag[0, :, 0]
    off = moduli_off[0, :, 0]
    low, high = pack(edge_kernel, "edge", 0.1, (diag, off), (HALF, HALF), 32)
    near = over(low, across)
    far = over(high, along)
    flow, low, high = lax.optimization_barrier((rate[0, 0], low, high))
    own = pack(
        pack_kernel, "pack", 0.1, (diag, off, schmid[0, :, 0], crss[0, :, 0], branch[0, 0], flow), (120,), 16
    )[0]
    other = over(own, partner)
    before, after, near, far, own = lax.optimization_barrier((before, after, near, far, own))
    core = member % 2

    where = member.reshape(1).astype(jnp.int32)
    message = call(
        strain_kernel,
        "strain",
        0.1,
        [SM, SM, SM, VM, VM, VM],
        [(8, LANES)],
        [pltpu.VMEM((3, 4, 32, LANES), F32)],
    )(point_node, point_owner, where, displacement, before, after)[0]
    rest_near = over(near, partner)
    rest_far = over(far, partner)
    message = jnp.broadcast_to(message[:groups, None, None, :], (groups, members, 1, LANES))
    arrived = lax.all_to_all(message.reshape(everyone, 1, LANES), both, 0, 0, tiled=True)
    strains = jnp.sum(arrived.reshape(groups, members, LANES), axis=1)
    ebar = [lax.dynamic_slice_in_dim(strains, core * PER_CORE + k, 1, axis=0) for k in range(PER_CORE)]

    base = stencil(stiffness, displacement, before, after, external)

    plane = (FIELDS, ROWS, LANES)
    packed = (2 * FIELDS, ROWS, LANES)
    temps = [pltpu.VMEM(plane, F32)] * 4
    side = core.reshape(1).astype(jnp.int32)
    ghosts = (near, far, rest_near, rest_far)
    ANY = pl.BlockSpec(memory_space=pl.ANY)
    x_0, x_1, own, other = call(
        fetch_kernel,
        "fetch",
        5,
        [SM] * 2 + [ANY] * 2 + [VM] * 4,
        [packed] * 2 + [(120, ROWS, LANES)] * 2,
        temps + [pltpu.SemaphoreType.DMA((4,))],
    )(side, ebar[0], *in_hbm(own, other), *ghosts)
    fixed = (own, other, *ghosts)
    state = [(x_0, x_1)]
    for k in range(1, PER_CORE):
        state.append(
            call(first_kernel, "first", 5, [SM] * 2 + [VM] * 6, [packed] * 2, temps)(side, ebar[k], *fixed)
        )
    sums = []
    for pair in range(4):
        for k in range(PER_CORE):
            x_0, x_1 = state[k]
            f_0 = over(x_1, rightward)
            f_1 = over(x_0, leftward)
            operands = (side, *fixed, x_0, x_1, f_0, f_1)
            if pair < 3:
                state[k] = call(pair_kernel, "pair", 5, [SM] + [VM] * 10, [packed] * 2, temps)(*operands)
            else:
                sizes = [pltpu.VMEM(packed, F32)] * 2 + temps
                sums += call(last_kernel, "last", 6, [SM] + [VM] * 10, [(FIELDS, CHUNK, LANES)], sizes)(*operands)

    totals = jnp.stack([jnp.sum(v, axis=(1, 2)) for v in lax.optimization_barrier(sums)])
    totals = jnp.pad(totals, ((0, 0), (0, LANES - 6)))
    mine = jnp.zeros((groups, LANES), F32)
    mine = lax.dynamic_update_slice_in_dim(mine, totals, core * PER_CORE, axis=0)
    reply = jnp.broadcast_to(mine[:, None, None, :], (groups, members, 1, LANES))
    received = lax.all_to_all(reply.reshape(everyone, 1, LANES), both, 0, 0, tiled=True)
    loads = jnp.pad(point_load.reshape(-1, 3, 6), ((0, 0), (0, 0), (0, LANES - 6)))
    residual, point_stress = call(
        final_kernel, "final", 2, [SM, SM, SM, VM, VM, VM], [(3, 2, 32, LANES), (2, 6)]
    )(point_node, point_owner, where, received.reshape(groups, members, LANES), loads, base)
    return (residual, point_stress)


def solution(mesh):
    in_specs = (
        P(None, ("grp", "rve"), None, None),
        P(None, None, None, ("grp", "rve"), None, None),
        P(None, ("grp", "rve"), None, None),
        P("grp"),
        P("grp", None),
        P("grp", None),
        P("grp", None, "rve", None, None),
        P("grp", None, "rve", None, None),
        P("grp", None, "rve", None, None),
        P("grp", None, "rve", None, None),
        P("grp", "rve", None, None),
        P("grp", "rve", None, None),
    )
    out_specs = (P(None, ("grp", "rve"), None, None), P("grp", None))
    return jax.shard_map(
        per_device, mesh=mesh, in_specs=in_specs, out_specs=out_specs, check_vma=False
    )
```

```python
import functools

import jax
import jax.numpy as jnp
from jax import lax
from jax.experimental import pallas as pl
from jax.experimental.pallas import tpu as pltpu
from jax.sharding import PartitionSpec as P

SLIP = 12
RELAX = 0.15
SHARE = RELAX / 6.0
ROWS = 64
LANES = 128
PER_CORE = 2
SLOTS = 1
FIELDS = SLOTS * 6
VMEM_LIMIT = 16 * 1024 * 1024
GROUP = 6
CHUNK = 16
HALF = 18
F32 = jnp.float32

VM = pl.BlockSpec(memory_space=pltpu.VMEM)
SM = pl.BlockSpec(memory_space=pltpu.SMEM)


def cost(micros):
    return pl.CostEstimate(flops=0, transcendentals=0, bytes_accessed=int(micros * 3.6e6))


def call(kernel, name, micros, in_specs, outs, scratch=()):
    return pl.pallas_call(
        kernel,
        name=name,
        in_specs=in_specs,
        out_specs=[VM] * len(outs),
        cost_estimate=cost(micros),
        out_shape=[jax.ShapeDtypeStruct(s, F32) for s in outs],
        scratch_shapes=list(scratch),
        compiler_params=pltpu.CompilerParams(vmem_limit_bytes=VMEM_LIMIT),
    )


def chunks(body):
    def step(k, carry):
        body(pl.ds(pl.multiple_of(k * CHUNK, CHUNK), CHUNK))
        return carry

    lax.fori_loop(0, ROWS // CHUNK, step, 0)


def pack_kernel(diag, off, schmid, crss, branch, rate, low, high, matrix, slips):
    for i in range(6):
        for j in range(6):
            k = 6 * i + j
            v = off[k] + diag[i] if i == j else off[k]
            matrix[k] = v
            if k < HALF:
                low[k] = v
            else:
                high[k - HALF] = v
    bits = branch[...]
    speed = rate[...]
    for a in range(SLIP):
        limit = crss[a]
        inverse = 1.0 / limit
        for j in range(6):
            slips[6 * a + j] = schmid[6 * a + j] * inverse
        active = (jnp.right_shift(bits, a) & 1).astype(F32)
        slips[6 * SLIP + a] = active * speed * (limit * limit)


def in_hbm(*arrays):
    return [pltpu.with_memory_space_constraint(v, pltpu.HBM) for v in arrays]


def pack(operands, planes, rows):
    block = lambda n: pl.BlockSpec((n, rows, LANES), lambda k: (0, k, 0))
    return pl.pallas_call(
        pack_kernel,
        name="pack",
        cost_estimate=cost(4),
        grid=(ROWS // rows,),
        in_specs=[
            block(v.shape[0]) if v.ndim == 3 else pl.BlockSpec((rows, LANES), lambda k: (k, 0))
            for v in operands
        ],
        out_specs=[block(n) for n in planes],
        out_shape=[jax.ShapeDtypeStruct((n, ROWS, LANES), F32) for n in planes],
        compiler_params=pltpu.CompilerParams(vmem_limit_bytes=VMEM_LIMIT),
    )(*in_hbm(*operands))


def times(c, at, vectors):
    sums = [[None] * 6 for _ in vectors]
    for i in range(6):
        for j in range(6):
            entry = c(6 * i + j, at)
            for s, vector in enumerate(vectors):
                term = entry * vector[j]
                sums[s][i] = term if j == 0 else sums[s][i] + term
    return sums


def load(ref, at):
    return [[ref[6 * s + i, at, :] for i in range(6)] for s in range(SLOTS)]


def store(ref, at, values):
    for s in range(SLOTS):
        for i in range(6):
            ref[6 * s + i, at, :] = values[s][i]


def slip(c, at, stress, total):
    total = [list(t) for t in total]
    for a in range(SLIP):
        rows = [c(36 + 6 * a + j, at) for j in range(6)]
        gain = c(108 + a, at)
        for s in range(SLOTS):
            t = rows[0] * stress[s][0]
            for j in range(1, 6):
                t = t + rows[j] * stress[s][j]
            w = gain * (t - jnp.tanh(t))
            for j in range(6):
                total[s][j] = total[s][j] - rows[j] * w
    return total


def around(x):
    rows = pltpu.roll(x, 1, axis=0) + pltpu.roll(x, ROWS - 1, axis=0)
    return rows + (pltpu.roll(x, 1, axis=1) + pltpu.roll(x, LANES - 1, axis=1))


def beside(sig_0, sig_1, base_0, base_1):
    def step(k, carry):
        for f in [k * GROUP + j for j in range(GROUP)]:
            u = sig_0[f]
            v = sig_1[f]
            base_0[f] = base_0[f] + SHARE * (around(u) + v)
            base_1[f] = base_1[f] + SHARE * (around(v) + u)
        return carry

    lax.fori_loop(0, FIELDS // GROUP, step, 0)


def combine(x, y, fn):
    return [[fn(x[s][i], y[s][i]) for i in range(6)] for s in range(SLOTS)]


def relaxed(e, sig):
    return combine(e, sig, lambda u, v: u - RELAX * v)


def whole(ref):
    return lambda k, at: ref[k, at, :]


def joined(low, high):
    return lambda k, at: low[k, at, :] if k < HALF else high[k - HALF, at, :]


def split(side, coefficients, run):
    own, other, near, far, rest_near, rest_far = coefficients
    early = joined(near, rest_far)
    late = joined(rest_near, far)
    pl.when(side[0] == 0)(lambda: run(whole(own), whole(other), early, late))
    pl.when(side[0] == 1)(lambda: run(whole(other), whole(own), late, early))


def zero_kernel(side, ebar, own_c, own_s, other_c, other_s, own, other, *refs):
    states, t_0, t_1, sems = refs[: 2 * PER_CORE], refs[-3], refs[-2], refs[-1]
    copies = [
        pltpu.make_async_copy(src, dst.at[low:high], sems.at[k])
        for k, (src, dst, low, high) in enumerate(
            (
                (own_c, own, 0, 36),
                (other_c, other, 0, 36),
                (own_s, own, 36, 120),
                (other_s, other, 36, 120),
            )
        )
    ]
    for copy in copies:
        copy.start()
    copies[0].wait()
    copies[1].wait()
    for k in range(PER_CORE):
        e_0, e_1 = states[2 * k : 2 * k + 2]

        def start(c_0, c_1, k=k, e_0=e_0, e_1=e_1):
            for c, t_ref, e_ref in ((c_0, t_0, e_0), (c_1, t_1, e_1)):

                def body(at, c=c, t_ref=t_ref, e_ref=e_ref):
                    strain = uniform(ebar, k)
                    sig = times(c, at, strain)
                    store(t_ref, at, sig)
                    store(e_ref, at, relaxed(strain, sig))

                chunks(body)

        def end(c_0, c_1, e_0=e_0, e_1=e_1):
            for c, t_ref, e_ref in ((c_0, t_0, e_0), (c_1, t_1, e_1)):

                def body(at, c=c, t_ref=t_ref, e_ref=e_ref):
                    store(e_ref, at, slip(c, at, load(t_ref, at), load(e_ref, at)))

                chunks(body)

        ordered(side, own, other, start)
        beside(t_0, t_1, e_0, e_1)
        if k == 0:
            copies[2].wait()
            copies[3].wait()
        ordered(side, own, other, end)


def ordered(side, own, other, run):
    pl.when(side[0] == 0)(lambda: run(whole(own), whole(other)))
    pl.when(side[0] == 1)(lambda: run(whole(other), whole(own)))


def uniform(ebar, k):
    return [[jnp.full((CHUNK, LANES), ebar[k, i], F32) for i in range(6)]]


def first_kernel(slot, side, ebar, own, other, near, far, rest_near, rest_far, e_0, e_1, x_0, x_1):
    def run(c_0, c_1, g_0, g_1):
        for c, g, e_ref, x_ref in ((c_0, g_0, e_0, x_0), (c_1, g_1, e_1, x_1)):

            def body(at, c=c, g=g, e_ref=e_ref, x_ref=x_ref):
                outer = times(g, at, uniform(ebar, slot))
                e = combine(load(e_ref, at), outer, lambda u, v: u + SHARE * v)
                onward(c, at, e, x_ref)

            chunks(body)

    split(side, (own, other, near, far, rest_near, rest_far), run)
    beside_own(x_0, x_1)


def onward(c, at, e, x_ref):
    sig = times(c, at, e)
    store(x_ref.at[0:FIELDS], at, sig)
    store(x_ref.at[FIELDS:], at, slip(c, at, sig, relaxed(e, sig)))


def advance(planes):
    for c, t_ref, e_ref, x_ref in planes:

        def body(at, c=c, t_ref=t_ref, e_ref=e_ref, x_ref=x_ref):
            onward(c, at, slip(c, at, load(t_ref, at), load(e_ref, at)), x_ref)

        chunks(body)


def beside_own(x_0, x_1):
    beside(x_0.at[0:FIELDS], x_1.at[0:FIELDS], x_0.at[FIELDS:], x_1.at[FIELDS:])


def arrive(planes):
    for x_ref, far_ref, c, g, t_ref, e_ref in planes:

        def body(at, x_ref=x_ref, far_ref=far_ref, c=c, g=g, t_ref=t_ref, e_ref=e_ref):
            add = lambda u, v: u + SHARE * v
            own = x_ref.at[0:FIELDS], x_ref.at[FIELDS:]
            far = far_ref.at[0:FIELDS], far_ref.at[FIELDS:]
            e = combine(load(own[1], at), load(far[0], at), add)
            sig = times(c, at, e)
            store(t_ref, at, sig)
            base = relaxed(e, sig)
            outer = times(g, at, combine(load(far[1], at), load(own[0], at), add))
            store(e_ref, at, combine(base, outer, add))

        chunks(body)


def two_sweeps(c_0, c_1, g_0, g_1, x_0, x_1, f_0, f_1, y_0, y_1, e_0, e_1, t_0, t_1):
    arrive(((x_0, f_0, c_0, g_0, t_0, e_0), (x_1, f_1, c_1, g_1, t_1, e_1)))
    beside(t_0, t_1, e_0, e_1)
    advance(((c_0, t_0, e_0, y_0), (c_1, t_1, e_1, y_1)))
    beside_own(y_0, y_1)


def pair_kernel(side, own, other, near, far, rest_near, rest_far, *refs):
    split(side, (own, other, near, far, rest_near, rest_far), lambda *c: two_sweeps(*c, *refs))


def last_kernel(side, own, other, near, far, rest_near, rest_far, x_0, x_1, f_0, f_1, out, y_0, y_1, *temps):
    def run(c_0, c_1, g_0, g_1):
        two_sweeps(c_0, c_1, g_0, g_1, x_0, x_1, f_0, f_1, y_0, y_1, *temps)
        for k in range(FIELDS):
            out[k] = jnp.zeros((CHUNK, LANES), F32)
        for y_ref, c, g in ((y_0, c_0, g_0), (y_1, c_1, g_1)):

            def body(at, y_ref=y_ref, c=c, g=g):
                mine = times(c, at, load(y_ref.at[FIELDS:], at))
                outer = times(g, at, load(y_ref.at[0:FIELDS], at))
                for s in range(SLOTS):
                    for i in range(6):
                        out[6 * s + i] = out[6 * s + i] + (mine[s][i] + SHARE * outer[s][i])

            chunks(body)

    split(side, (own, other, near, far, rest_near, rest_far), run)


def strain_kernel(node, owner, member, disp, before, after, out, grid):
    grid[:, 0:1] = before[...]
    grid[:, 1:3] = disp[...]
    grid[:, 3:4] = after[...]
    lane = lax.broadcasted_iota(jnp.int32, (1, LANES), 1)
    group = lax.broadcasted_iota(jnp.int32, (8, LANES), 0)
    total = jnp.zeros((8, LANES), F32)
    for p in range(2):
        local = node[p] - member[0] * (2 * 32 * LANES)
        present = (local >= 0) & (local < 2 * 32 * LANES)
        local = jnp.clip(local, 0, 2 * 32 * LANES - 1)
        x = local // (32 * LANES)
        y = (local // LANES) % 32
        z = local % LANES
        up_y = jnp.minimum(y + 1, 31)
        down_y = jnp.maximum(y - 1, 0)
        has_up = jnp.where(y < 31, 1.0, 0.0).astype(F32)
        has_down = jnp.where(y > 0, 1.0, 0.0).astype(F32)
        slope = []
        for c in range(3):
            row = lambda dx, yy: grid[c, x + dx, pl.ds(yy, 1), :]
            gx = (row(2, y) - row(0, y)) * 0.5
            gy = (row(1, up_y) * has_up - row(1, down_y) * has_down) * 0.5
            mid = row(1, y)
            right = jnp.where(lane < LANES - 1, pltpu.roll(mid, LANES - 1, axis=1), 0.0)
            left = jnp.where(lane > 0, pltpu.roll(mid, 1, axis=1), 0.0)
            slope.append((gx, gy, (right - left) * 0.5))
        parts = [
            slope[0][0],
            slope[1][1],
            slope[2][2],
            slope[1][2] + slope[2][1],
            slope[0][2] + slope[2][0],
            slope[0][1] + slope[1][0],
        ]
        here = (lane == z) & present
        line = jnp.zeros((1, LANES), F32)
        for j, part in enumerate(parts):
            value = jnp.sum(jnp.where(here, part, 0.0), axis=1, keepdims=True)
            line = line + jnp.where(lane == j, value, 0.0)
        total = total + jnp.where(group == owner[p, 0], line, 0.0)
    out[...] = total


def stencil_kernel(blocks, disp, before, after, external, out, moved, total):
    step = pl.program_id(0)

    @pl.when(step == 0)
    def _():
        lane = lax.broadcasted_iota(jnp.int32, (32, LANES), 1)
        row = lax.broadcasted_iota(jnp.int32, (32, LANES), 0)
        total[...] = jnp.zeros_like(total)
        for c in range(3):
            for x in range(4):
                v = before[c, 0] if x == 0 else (after[c, 0] if x == 3 else disp[c, x - 1])
                for j in range(3):
                    w = v
                    if j == 0:
                        w = jnp.where(row > 0, pltpu.roll(v, 1, axis=0), 0.0)
                    if j == 2:
                        w = jnp.where(row < 31, pltpu.roll(v, 31, axis=0), 0.0)
                    moved[j, 0, c, x] = jnp.where(lane > 0, pltpu.roll(w, 1, axis=1), 0.0)
                    moved[j, 1, c, x] = w
                    moved[j, 2, c, x] = jnp.where(lane < LANES - 1, pltpu.roll(w, LANES - 1, axis=1), 0.0)

    i = step // 3
    j = step % 3
    for c in range(3):
        for x in range(2):
            s = total[c, x]
            for k in range(3):
                for d in range(3):
                    s = s + blocks[k, c, d, x].astype(F32) * moved[j, k, d, i + x]
            total[c, x] = s

    @pl.when(step == 8)
    def _():
        out[...] = external[...] - total[...]


def stencil(stiffness, disp, before, after, external):
    whole = lambda n: pl.BlockSpec((3, n, 32, LANES), lambda s: (0, 0, 0, 0))
    return pl.pallas_call(
        stencil_kernel,
        name="stencil",
        cost_estimate=cost(5),
        grid=(9,),
        in_specs=[
            pl.BlockSpec((3, 3, 3, 2, 32, LANES), lambda s: (s, 0, 0, 0, 0, 0)),
            whole(2),
            whole(1),
            whole(1),
            whole(2),
        ],
        out_specs=whole(2),
        out_shape=jax.ShapeDtypeStruct((3, 2, 32, LANES), F32),
        scratch_shapes=[
            pltpu.VMEM((3, 3, 3, 4, 32, LANES), F32),
            pltpu.VMEM((3, 2, 32, LANES), F32),
        ],
        compiler_params=pltpu.CompilerParams(vmem_limit_bytes=VMEM_LIMIT),
    )(*in_hbm(stiffness, disp, before, after, external))


def final_kernel(node, owner, member, received, loads, base, residual, stress):
    residual[...] = base[...]
    lane = lax.broadcasted_iota(jnp.int32, (1, LANES), 1)
    sums = [jnp.sum(received[g], axis=0, keepdims=True) for g in range(4)]
    for p in range(2):
        line = jnp.zeros((1, LANES), F32)
        for g in range(4):
            line = line + jnp.where(owner[p, 0] == g, sums[g], 0.0)
        line = line * (1.0 / 262144.0)
        stress[p : p + 1, :] = line[:, 0:6]
        local = node[p] - member[0] * (2 * 32 * LANES)
        present = (local >= 0) & (local < 2 * 32 * LANES)
        local = jnp.clip(local, 0, 2 * 32 * LANES - 1)
        x = local // (32 * LANES)
        y = (local // LANES) % 32
        z = local % LANES
        here = (lane == z) & present
        for c in range(3):
            force = jnp.sum(loads[p, c : c + 1, :] * line, axis=1, keepdims=True)
            row = residual[c, x, pl.ds(y, 1), :]
            residual[c, x, pl.ds(y, 1), :] = row - jnp.where(here, force, 0.0)


def per_device(
    displacement,
    stiffness,
    external,
    point_node,
    point_owner,
    point_load,
    moduli_diag,
    moduli_off,
    schmid,
    crss,
    branch,
    rate,
):
    groups = lax.axis_size("grp")
    members = lax.axis_size("rve")
    member = lax.axis_index("rve")
    everyone = groups * members

    def over(value, pairs, axis="rve"):
        return lax.ppermute(value, axis, pairs)

    partner = [(i, i ^ 1) for i in range(members)]
    across = [(i, (i - 1 if i % 2 == 0 else i + 1) % members) for i in range(members)]
    along = [(i, (i - 2 if i % 2 == 0 else i + 2) % members) for i in range(members)]
    rightward = [(i, (i + 2) % members) for i in range(members)]
    leftward = [(i, (i - 2) % members) for i in range(members)]

    both = ("grp", "rve")
    upward = [(i, i + 1) for i in range(everyone - 1)]
    downward = [(i + 1, i) for i in range(everyone - 1)]
    before = over(displacement[:, 1:2], upward, both)
    after = over(displacement[:, 0:1], downward, both)

    low, high, *own = pack(
        (moduli_diag[0, :, 0], moduli_off[0, :, 0], schmid[0, :, 0], crss[0, :, 0], branch[0, 0], rate[0, 0]),
        (HALF, HALF, 36, 84),
        32,
    )
    before, after, low, high, own = lax.optimization_barrier((before, after, low, high, own))
    near = over(low, across)
    far = over(high, along)
    other = [over(v, partner) for v in own]
    core = member % 2

    where = member.reshape(1).astype(jnp.int32)
    message = call(
        strain_kernel,
        "strain",
        0.1,
        [SM, SM, SM, VM, VM, VM],
        [(8, LANES)],
        [pltpu.VMEM((3, 4, 32, LANES), F32)],
    )(point_node, point_owner, where, displacement, before, after)[0]
    message = jnp.broadcast_to(message[:groups, None, None, :], (groups, members, 1, LANES))
    arrived = lax.all_to_all(message.reshape(everyone, 1, LANES), both, 0, 0, tiled=True)
    near, far, arrived = lax.optimization_barrier((near, far, arrived))
    rest_near = over(near, partner)
    rest_far = over(far, partner)
    strains = jnp.sum(arrived.reshape(groups, members, LANES), axis=1)
    ebar = lax.dynamic_slice_in_dim(strains, core * PER_CORE, PER_CORE, axis=0)

    base = stencil(stiffness, displacement, before, after, external)

    plane = (FIELDS, ROWS, LANES)
    packed = (2 * FIELDS, ROWS, LANES)
    temps = [pltpu.VMEM(plane, F32)] * 4
    side = core.reshape(1).astype(jnp.int32)
    ghosts = (near, far, rest_near, rest_far)
    ANY = pl.BlockSpec(memory_space=pl.ANY)
    outs = call(
        zero_kernel,
        "zero",
        5,
        [SM] * 2 + [ANY] * 4,
        [(120, ROWS, LANES)] * 2 + [plane] * (2 * PER_CORE),
        temps[:2] + [pltpu.SemaphoreType.DMA((4,))],
    )(side, ebar, *in_hbm(*own, *other))
    fixed = (*outs[:2], *ghosts)
    state = []
    for k in range(PER_CORE):
        kernel = functools.partial(first_kernel, k)
        state.append(
            call(kernel, "first", 5, [SM] * 2 + [VM] * 8, [packed] * 2)(
                side, ebar, *fixed, *outs[2 + 2 * k : 4 + 2 * k]
            )
        )
    sums = []
    for pair in range(4):
        for k in range(PER_CORE):
            x_0, x_1 = state[k]
            f_0 = over(x_1, rightward)
            f_1 = over(x_0, leftward)
            operands = (side, *fixed, x_0, x_1, f_0, f_1)
            if pair < 3:
                state[k] = call(pair_kernel, "pair", 5, [SM] + [VM] * 10, [packed] * 2, temps)(*operands)
            else:
                sizes = [pltpu.VMEM(packed, F32)] * 2 + temps
                sums += call(last_kernel, "last", 6, [SM] + [VM] * 10, [(FIELDS, CHUNK, LANES)], sizes)(*operands)

    totals = jnp.stack([jnp.sum(v, axis=(1, 2)) for v in lax.optimization_barrier(sums)])
    totals = jnp.pad(totals, ((0, 0), (0, LANES - 6)))
    mine = jnp.zeros((groups, LANES), F32)
    mine = lax.dynamic_update_slice_in_dim(mine, totals, core * PER_CORE, axis=0)
    reply = jnp.broadcast_to(mine[:, None, None, :], (groups, members, 1, LANES))
    received = lax.all_to_all(reply.reshape(everyone, 1, LANES), both, 0, 0, tiled=True)
    loads = jnp.pad(point_load.reshape(-1, 3, 6), ((0, 0), (0, 0), (0, LANES - 6)))
    residual, point_stress = call(
        final_kernel, "final", 2, [SM, SM, SM, VM, VM, VM], [(3, 2, 32, LANES), (2, 6)]
    )(point_node, point_owner, where, received.reshape(groups, members, LANES), loads, base)
    return (residual, point_stress)


def solution(mesh):
    in_specs = (
        P(None, ("grp", "rve"), None, None),
        P(None, None, None, ("grp", "rve"), None, None),
        P(None, ("grp", "rve"), None, None),
        P("grp"),
        P("grp", None),
        P("grp", None),
        P("grp", None, "rve", None, None),
        P("grp", None, "rve", None, None),
        P("grp", None, "rve", None, None),
        P("grp", None, "rve", None, None),
        P("grp", "rve", None, None),
        P("grp", "rve", None, None),
    )
    out_specs = (P(None, ("grp", "rve"), None, None), P("grp", None))
    return jax.shard_map(
        per_device, mesh=mesh, in_specs=in_specs, out_specs=out_specs, check_vma=False
    )
```

```python
import functools

import jax
import jax.numpy as jnp
from jax import lax
from jax.experimental import pallas as pl
from jax.experimental.pallas import tpu as pltpu
from jax.sharding import PartitionSpec as P

SLIP = 12
RELAX = 0.15
SHARE = RELAX / 6.0
ROWS = 64
LANES = 128
PER_CORE = 2
FIRST = 1
SLOTS = 1
FIELDS = SLOTS * 6
VMEM_LIMIT = 16 * 1024 * 1024
GROUP = 6
CHUNK = 16
HALF = 18
F32 = jnp.float32

VM = pl.BlockSpec(memory_space=pltpu.VMEM)
SM = pl.BlockSpec(memory_space=pltpu.SMEM)


def cost(micros):
    return pl.CostEstimate(flops=0, transcendentals=0, bytes_accessed=int(micros * 3.6e6))


def call(kernel, name, micros, in_specs, outs, scratch=()):
    return pl.pallas_call(
        kernel,
        name=name,
        in_specs=in_specs,
        out_specs=[VM] * len(outs),
        cost_estimate=cost(micros),
        out_shape=[jax.ShapeDtypeStruct(s, F32) for s in outs],
        scratch_shapes=list(scratch),
        compiler_params=pltpu.CompilerParams(vmem_limit_bytes=VMEM_LIMIT),
    )


def chunks(body):
    def step(k, carry):
        body(pl.ds(pl.multiple_of(k * CHUNK, CHUNK), CHUNK))
        return carry

    lax.fori_loop(0, ROWS // CHUNK, step, 0)


def pack_kernel(diag, off, schmid, crss, branch, rate, low, high, matrix, slips):
    for i in range(6):
        for j in range(6):
            k = 6 * i + j
            v = off[k] + diag[i] if i == j else off[k]
            matrix[k] = v
            if k < HALF:
                low[k] = v
            else:
                high[k - HALF] = v
    bits = branch[...]
    speed = rate[...]
    for a in range(SLIP):
        limit = crss[a]
        inverse = 1.0 / limit
        for j in range(6):
            slips[6 * a + j] = schmid[6 * a + j] * inverse
        active = (jnp.right_shift(bits, a) & 1).astype(F32)
        slips[6 * SLIP + a] = active * speed * (limit * limit)


def in_hbm(*arrays):
    return [pltpu.with_memory_space_constraint(v, pltpu.HBM) for v in arrays]


def pack(operands, planes, rows):
    block = lambda n: pl.BlockSpec((n, rows, LANES), lambda k: (0, k, 0))
    return pl.pallas_call(
        pack_kernel,
        name="pack",
        cost_estimate=cost(4),
        grid=(ROWS // rows,),
        in_specs=[
            block(v.shape[0]) if v.ndim == 3 else pl.BlockSpec((rows, LANES), lambda k: (k, 0))
            for v in operands
        ],
        out_specs=[block(n) for n in planes],
        out_shape=[jax.ShapeDtypeStruct((n, ROWS, LANES), F32) for n in planes],
        compiler_params=pltpu.CompilerParams(vmem_limit_bytes=VMEM_LIMIT),
    )(*in_hbm(*operands))


def times(c, at, vectors):
    sums = [[None] * 6 for _ in vectors]
    for i in range(6):
        for j in range(6):
            entry = c(6 * i + j, at)
            for s, vector in enumerate(vectors):
                term = entry * vector[j]
                sums[s][i] = term if j == 0 else sums[s][i] + term
    return sums


def load(ref, at):
    return [[ref[6 * s + i, at, :] for i in range(6)] for s in range(SLOTS)]


def store(ref, at, values):
    for s in range(SLOTS):
        for i in range(6):
            ref[6 * s + i, at, :] = values[s][i]


def slip(c, at, stress, total):
    total = [list(t) for t in total]
    for a in range(SLIP):
        rows = [c(36 + 6 * a + j, at) for j in range(6)]
        gain = c(108 + a, at)
        for s in range(SLOTS):
            t = rows[0] * stress[s][0]
            for j in range(1, 6):
                t = t + rows[j] * stress[s][j]
            w = gain * (t - jnp.tanh(t))
            for j in range(6):
                total[s][j] = total[s][j] - rows[j] * w
    return total


def around(x):
    rows = pltpu.roll(x, 1, axis=0) + pltpu.roll(x, ROWS - 1, axis=0)
    return rows + (pltpu.roll(x, 1, axis=1) + pltpu.roll(x, LANES - 1, axis=1))


def beside(sig_0, sig_1, base_0, base_1):
    def step(k, carry):
        for f in [k * GROUP + j for j in range(GROUP)]:
            u = sig_0[f]
            v = sig_1[f]
            base_0[f] = base_0[f] + SHARE * (around(u) + v)
            base_1[f] = base_1[f] + SHARE * (around(v) + u)
        return carry

    lax.fori_loop(0, FIELDS // GROUP, step, 0)


def combine(x, y, fn):
    return [[fn(x[s][i], y[s][i]) for i in range(6)] for s in range(SLOTS)]


def relaxed(e, sig):
    return combine(e, sig, lambda u, v: u - RELAX * v)


def whole(ref):
    return lambda k, at: ref[k, at, :]


def joined(low, high):
    return lambda k, at: low[k, at, :] if k < HALF else high[k - HALF, at, :]


def split(side, coefficients, run):
    own, other, near, far, rest_near, rest_far = coefficients
    early = joined(near, rest_far)
    late = joined(rest_near, far)
    pl.when(side[0] == 0)(lambda: run(whole(own), whole(other), early, late))
    pl.when(side[0] == 1)(lambda: run(whole(other), whole(own), late, early))


def zero_kernel(side, ebar, own_c, own_s, other_c, other_s, own, other, *refs):
    t_0, t_1, sems = refs[2:]
    copies = [
        pltpu.make_async_copy(src, dst.at[low:high], sems.at[k])
        for k, (src, dst, low, high) in enumerate(
            (
                (own_c, own, 0, 36),
                (other_c, other, 0, 36),
                (own_s, own, 36, 120),
                (other_s, other, 36, 120),
            )
        )
    ]
    for copy in copies:
        copy.start()
    copies[0].wait()
    copies[1].wait()
    ready = lambda: (copies[2].wait(), copies[3].wait())
    zero_sweep(side, ebar, FIRST, own, other, *refs[:2], t_0, t_1, ready)


def entire_kernel(slot, side, ebar, own, other, near, far, rest_near, rest_far, x_0, x_1, e_0, e_1, t_0, t_1):
    zero_sweep(side, ebar, slot, own, other, e_0, e_1, t_0, t_1, lambda: None)
    first_kernel(slot, side, ebar, own, other, near, far, rest_near, rest_far, e_0, e_1, x_0, x_1)


def zero_sweep(side, ebar, slot, own, other, e_0, e_1, t_0, t_1, ready):
    def start(c_0, c_1):
        for c, t_ref, e_ref in ((c_0, t_0, e_0), (c_1, t_1, e_1)):

            def body(at, c=c, t_ref=t_ref, e_ref=e_ref):
                strain = uniform(ebar, slot)
                sig = times(c, at, strain)
                store(t_ref, at, sig)
                store(e_ref, at, relaxed(strain, sig))

            chunks(body)

    def end(c_0, c_1):
        for c, t_ref, e_ref in ((c_0, t_0, e_0), (c_1, t_1, e_1)):

            def body(at, c=c, t_ref=t_ref, e_ref=e_ref):
                store(e_ref, at, slip(c, at, load(t_ref, at), load(e_ref, at)))

            chunks(body)

    ordered(side, own, other, start)
    beside(t_0, t_1, e_0, e_1)
    ready()
    ordered(side, own, other, end)


def ordered(side, own, other, run):
    pl.when(side[0] == 0)(lambda: run(whole(own), whole(other)))
    pl.when(side[0] == 1)(lambda: run(whole(other), whole(own)))


def uniform(ebar, k):
    return [[jnp.full((CHUNK, LANES), ebar[k, i], F32) for i in range(6)]]


def first_kernel(slot, side, ebar, own, other, near, far, rest_near, rest_far, e_0, e_1, x_0, x_1):
    def run(c_0, c_1, g_0, g_1):
        for c, g, e_ref, x_ref in ((c_0, g_0, e_0, x_0), (c_1, g_1, e_1, x_1)):

            def body(at, c=c, g=g, e_ref=e_ref, x_ref=x_ref):
                outer = times(g, at, uniform(ebar, slot))
                e = combine(load(e_ref, at), outer, lambda u, v: u + SHARE * v)
                onward(c, at, e, x_ref)

            chunks(body)

    split(side, (own, other, near, far, rest_near, rest_far), run)
    beside_own(x_0, x_1)


def onward(c, at, e, x_ref):
    sig = times(c, at, e)
    store(x_ref.at[0:FIELDS], at, sig)
    store(x_ref.at[FIELDS:], at, slip(c, at, sig, relaxed(e, sig)))


def advance(planes):
    for c, t_ref, e_ref, x_ref in planes:

        def body(at, c=c, t_ref=t_ref, e_ref=e_ref, x_ref=x_ref):
            onward(c, at, slip(c, at, load(t_ref, at), load(e_ref, at)), x_ref)

        chunks(body)


def beside_own(x_0, x_1):
    beside(x_0.at[0:FIELDS], x_1.at[0:FIELDS], x_0.at[FIELDS:], x_1.at[FIELDS:])


def arrive(planes):
    for x_ref, far_ref, c, g, t_ref, e_ref in planes:

        def body(at, x_ref=x_ref, far_ref=far_ref, c=c, g=g, t_ref=t_ref, e_ref=e_ref):
            add = lambda u, v: u + SHARE * v
            own = x_ref.at[0:FIELDS], x_ref.at[FIELDS:]
            far = far_ref.at[0:FIELDS], far_ref.at[FIELDS:]
            e = combine(load(own[1], at), load(far[0], at), add)
            sig = times(c, at, e)
            store(t_ref, at, sig)
            base = relaxed(e, sig)
            outer = times(g, at, combine(load(far[1], at), load(own[0], at), add))
            store(e_ref, at, combine(base, outer, add))

        chunks(body)


def two_sweeps(c_0, c_1, g_0, g_1, x_0, x_1, f_0, f_1, y_0, y_1, e_0, e_1, t_0, t_1):
    arrive(((x_0, f_0, c_0, g_0, t_0, e_0), (x_1, f_1, c_1, g_1, t_1, e_1)))
    beside(t_0, t_1, e_0, e_1)
    advance(((c_0, t_0, e_0, y_0), (c_1, t_1, e_1, y_1)))
    beside_own(y_0, y_1)


def pair_kernel(side, own, other, near, far, rest_near, rest_far, *refs):
    split(side, (own, other, near, far, rest_near, rest_far), lambda *c: two_sweeps(*c, *refs))


def last_kernel(side, own, other, near, far, rest_near, rest_far, x_0, x_1, f_0, f_1, out, y_0, y_1, *temps):
    def run(c_0, c_1, g_0, g_1):
        two_sweeps(c_0, c_1, g_0, g_1, x_0, x_1, f_0, f_1, y_0, y_1, *temps)
        for k in range(FIELDS):
            out[k] = jnp.zeros((CHUNK, LANES), F32)
        for y_ref, c, g in ((y_0, c_0, g_0), (y_1, c_1, g_1)):

            def body(at, y_ref=y_ref, c=c, g=g):
                mine = times(c, at, load(y_ref.at[FIELDS:], at))
                outer = times(g, at, load(y_ref.at[0:FIELDS], at))
                for s in range(SLOTS):
                    for i in range(6):
                        out[6 * s + i] = out[6 * s + i] + (mine[s][i] + SHARE * outer[s][i])

            chunks(body)

    split(side, (own, other, near, far, rest_near, rest_far), run)


def strain_kernel(node, owner, member, disp, before, after, out, grid):
    grid[:, 0:1] = before[...]
    grid[:, 1:3] = disp[...]
    grid[:, 3:4] = after[...]
    lane = lax.broadcasted_iota(jnp.int32, (1, LANES), 1)
    group = lax.broadcasted_iota(jnp.int32, (8, LANES), 0)
    total = jnp.zeros((8, LANES), F32)
    for p in range(2):
        local = node[p] - member[0] * (2 * 32 * LANES)
        present = (local >= 0) & (local < 2 * 32 * LANES)
        local = jnp.clip(local, 0, 2 * 32 * LANES - 1)
        x = local // (32 * LANES)
        y = (local // LANES) % 32
        z = local % LANES
        up_y = jnp.minimum(y + 1, 31)
        down_y = jnp.maximum(y - 1, 0)
        has_up = jnp.where(y < 31, 1.0, 0.0).astype(F32)
        has_down = jnp.where(y > 0, 1.0, 0.0).astype(F32)
        slope = []
        for c in range(3):
            row = lambda dx, yy: grid[c, x + dx, pl.ds(yy, 1), :]
            gx = (row(2, y) - row(0, y)) * 0.5
            gy = (row(1, up_y) * has_up - row(1, down_y) * has_down) * 0.5
            mid = row(1, y)
            right = jnp.where(lane < LANES - 1, pltpu.roll(mid, LANES - 1, axis=1), 0.0)
            left = jnp.where(lane > 0, pltpu.roll(mid, 1, axis=1), 0.0)
            slope.append((gx, gy, (right - left) * 0.5))
        parts = [
            slope[0][0],
            slope[1][1],
            slope[2][2],
            slope[1][2] + slope[2][1],
            slope[0][2] + slope[2][0],
            slope[0][1] + slope[1][0],
        ]
        here = (lane == z) & present
        line = jnp.zeros((1, LANES), F32)
        for j, part in enumerate(parts):
            value = jnp.sum(jnp.where(here, part, 0.0), axis=1, keepdims=True)
            line = line + jnp.where(lane == j, value, 0.0)
        total = total + jnp.where(group == owner[p, 0], line, 0.0)
    out[...] = total


def stencil_kernel(blocks, disp, before, after, external, out, moved, total):
    step = pl.program_id(0)

    @pl.when(step == 0)
    def _():
        lane = lax.broadcasted_iota(jnp.int32, (32, LANES), 1)
        row = lax.broadcasted_iota(jnp.int32, (32, LANES), 0)
        total[...] = jnp.zeros_like(total)
        for c in range(3):
            for x in range(4):
                v = before[c, 0] if x == 0 else (after[c, 0] if x == 3 else disp[c, x - 1])
                for j in range(3):
                    w = v
                    if j == 0:
                        w = jnp.where(row > 0, pltpu.roll(v, 1, axis=0), 0.0)
                    if j == 2:
                        w = jnp.where(row < 31, pltpu.roll(v, 31, axis=0), 0.0)
                    moved[j, 0, c, x] = jnp.where(lane > 0, pltpu.roll(w, 1, axis=1), 0.0)
                    moved[j, 1, c, x] = w
                    moved[j, 2, c, x] = jnp.where(lane < LANES - 1, pltpu.roll(w, LANES - 1, axis=1), 0.0)

    i = step // 3
    j = step % 3
    for c in range(3):
        for x in range(2):
            s = total[c, x]
            for k in range(3):
                for d in range(3):
                    s = s + blocks[k, c, d, x].astype(F32) * moved[j, k, d, i + x]
            total[c, x] = s

    @pl.when(step == 8)
    def _():
        out[...] = external[...] - total[...]


def stencil(stiffness, disp, before, after, external):
    whole = lambda n: pl.BlockSpec((3, n, 32, LANES), lambda s: (0, 0, 0, 0))
    return pl.pallas_call(
        stencil_kernel,
        name="stencil",
        cost_estimate=cost(5),
        grid=(9,),
        in_specs=[
            pl.BlockSpec((3, 3, 3, 2, 32, LANES), lambda s: (s, 0, 0, 0, 0, 0)),
            whole(2),
            whole(1),
            whole(1),
            whole(2),
        ],
        out_specs=whole(2),
        out_shape=jax.ShapeDtypeStruct((3, 2, 32, LANES), F32),
        scratch_shapes=[
            pltpu.VMEM((3, 3, 3, 4, 32, LANES), F32),
            pltpu.VMEM((3, 2, 32, LANES), F32),
        ],
        compiler_params=pltpu.CompilerParams(vmem_limit_bytes=VMEM_LIMIT),
    )(*in_hbm(stiffness, disp, before, after, external))


def final_kernel(node, owner, member, received, loads, base, residual, stress):
    residual[...] = base[...]
    lane = lax.broadcasted_iota(jnp.int32, (1, LANES), 1)
    sums = [jnp.sum(received[g], axis=0, keepdims=True) for g in range(4)]
    for p in range(2):
        line = jnp.zeros((1, LANES), F32)
        for g in range(4):
            line = line + jnp.where(owner[p, 0] == g, sums[g], 0.0)
        line = line * (1.0 / 262144.0)
        stress[p : p + 1, :] = line[:, 0:6]
        local = node[p] - member[0] * (2 * 32 * LANES)
        present = (local >= 0) & (local < 2 * 32 * LANES)
        local = jnp.clip(local, 0, 2 * 32 * LANES - 1)
        x = local // (32 * LANES)
        y = (local // LANES) % 32
        z = local % LANES
        here = (lane == z) & present
        for c in range(3):
            force = jnp.sum(loads[p, c : c + 1, :] * line, axis=1, keepdims=True)
            row = residual[c, x, pl.ds(y, 1), :]
            residual[c, x, pl.ds(y, 1), :] = row - jnp.where(here, force, 0.0)


def per_device(
    displacement,
    stiffness,
    external,
    point_node,
    point_owner,
    point_load,
    moduli_diag,
    moduli_off,
    schmid,
    crss,
    branch,
    rate,
):
    groups = lax.axis_size("grp")
    members = lax.axis_size("rve")
    member = lax.axis_index("rve")
    everyone = groups * members

    def over(value, pairs, axis="rve"):
        return lax.ppermute(value, axis, pairs)

    partner = [(i, i ^ 1) for i in range(members)]
    across = [(i, (i - 1 if i % 2 == 0 else i + 1) % members) for i in range(members)]
    along = [(i, (i - 2 if i % 2 == 0 else i + 2) % members) for i in range(members)]
    rightward = [(i, (i + 2) % members) for i in range(members)]
    leftward = [(i, (i - 2) % members) for i in range(members)]

    both = ("grp", "rve")
    upward = [(i, i + 1) for i in range(everyone - 1)]
    downward = [(i + 1, i) for i in range(everyone - 1)]
    before = over(displacement[:, 1:2], upward, both)
    after = over(displacement[:, 0:1], downward, both)

    low, high, *own = pack(
        (moduli_diag[0, :, 0], moduli_off[0, :, 0], schmid[0, :, 0], crss[0, :, 0], branch[0, 0], rate[0, 0]),
        (HALF, HALF, 36, 84),
        32,
    )
    before, after, low, high, own = lax.optimization_barrier((before, after, low, high, own))
    near = over(low, across)
    far = over(high, along)
    other = [over(v, partner) for v in own]
    core = member % 2

    where = member.reshape(1).astype(jnp.int32)
    message = call(
        strain_kernel,
        "strain",
        0.1,
        [SM, SM, SM, VM, VM, VM],
        [(8, LANES)],
        [pltpu.VMEM((3, 4, 32, LANES), F32)],
    )(point_node, point_owner, where, displacement, before, after)[0]
    message = jnp.broadcast_to(message[:groups, None, None, :], (groups, members, 1, LANES))
    arrived = lax.all_to_all(message.reshape(everyone, 1, LANES), both, 0, 0, tiled=True)
    near, far, arrived = lax.optimization_barrier((near, far, arrived))
    rest_near = over(near, partner)
    rest_far = over(far, partner)
    strains = jnp.sum(arrived.reshape(groups, members, LANES), axis=1)
    ebar = lax.dynamic_slice_in_dim(strains, core * PER_CORE, PER_CORE, axis=0)

    base = stencil(stiffness, displacement, before, after, external)

    plane = (FIELDS, ROWS, LANES)
    packed = (2 * FIELDS, ROWS, LANES)
    temps = [pltpu.VMEM(plane, F32)] * 4
    side = core.reshape(1).astype(jnp.int32)
    ghosts = (near, far, rest_near, rest_far)
    ANY = pl.BlockSpec(memory_space=pl.ANY)
    outs = call(
        zero_kernel,
        "zero",
        5,
        [SM] * 2 + [ANY] * 4,
        [(120, ROWS, LANES)] * 2 + [plane] * 2,
        temps[:2] + [pltpu.SemaphoreType.DMA((4,))],
    )(side, ebar, *in_hbm(*own, *other))
    fixed = (*outs[:2], *ghosts)
    state = [None] * PER_CORE
    for k in range(PER_CORE):
        if k == FIRST:
            kernel = functools.partial(first_kernel, k)
            state[k] = call(kernel, "first", 5, [SM] * 2 + [VM] * 8, [packed] * 2)(side, ebar, *fixed, *outs[2:])
        else:
            kernel = functools.partial(entire_kernel, k)
            state[k] = call(kernel, "entire", 5, [SM] * 2 + [VM] * 6, [packed] * 2, temps)(side, ebar, *fixed)
    sums = []
    for pair in range(4):
        for k in range(PER_CORE):
            x_0, x_1 = state[k]
            f_0 = over(x_1, rightward)
            f_1 = over(x_0, leftward)
            operands = (side, *fixed, x_0, x_1, f_0, f_1)
            if pair < 3:
                state[k] = call(pair_kernel, "pair", 5, [SM] + [VM] * 10, [packed] * 2, temps)(*operands)
            else:
                sizes = [pltpu.VMEM(packed, F32)] * 2 + temps
                sums += call(last_kernel, "last", 6, [SM] + [VM] * 10, [(FIELDS, CHUNK, LANES)], sizes)(*operands)

    totals = jnp.stack([jnp.sum(v, axis=(1, 2)) for v in lax.optimization_barrier(sums)])
    totals = jnp.pad(totals, ((0, 0), (0, LANES - 6)))
    mine = jnp.zeros((groups, LANES), F32)
    mine = lax.dynamic_update_slice_in_dim(mine, totals, core * PER_CORE, axis=0)
    reply = jnp.broadcast_to(mine[:, None, None, :], (groups, members, 1, LANES))
    received = lax.all_to_all(reply.reshape(everyone, 1, LANES), both, 0, 0, tiled=True)
    loads = jnp.pad(point_load.reshape(-1, 3, 6), ((0, 0), (0, 0), (0, LANES - 6)))
    residual, point_stress = call(
        final_kernel, "final", 2, [SM, SM, SM, VM, VM, VM], [(3, 2, 32, LANES), (2, 6)]
    )(point_node, point_owner, where, received.reshape(groups, members, LANES), loads, base)
    return (residual, point_stress)


def solution(mesh):
    in_specs = (
        P(None, ("grp", "rve"), None, None),
        P(None, None, None, ("grp", "rve"), None, None),
        P(None, ("grp", "rve"), None, None),
        P("grp"),
        P("grp", None),
        P("grp", None),
        P("grp", None, "rve", None, None),
        P("grp", None, "rve", None, None),
        P("grp", None, "rve", None, None),
        P("grp", None, "rve", None, None),
        P("grp", "rve", None, None),
        P("grp", "rve", None, None),
    )
    out_specs = (P(None, ("grp", "rve"), None, None), P("grp", None))
    return jax.shard_map(
        per_device, mesh=mesh, in_specs=in_specs, out_specs=out_specs, check_vma=False
    )
```

```python
import functools

import jax
import jax.numpy as jnp
from jax import lax
from jax.experimental import pallas as pl
from jax.experimental.pallas import tpu as pltpu
from jax.sharding import PartitionSpec as P

SLIP = 12
RELAX = 0.15
SHARE = RELAX / 6.0
ROWS = 64
LANES = 128
PER_CORE = 2
FIRST = 1
SLOTS = 1
FIELDS = SLOTS * 6
VMEM_LIMIT = 16 * 1024 * 1024
GROUP = 6
CHUNK = 16
HALF = 18
F32 = jnp.float32

VM = pl.BlockSpec(memory_space=pltpu.VMEM)
SM = pl.BlockSpec(memory_space=pltpu.SMEM)


def cost(micros):
    return pl.CostEstimate(flops=0, transcendentals=0, bytes_accessed=int(micros * 3.6e6))


def call(kernel, name, micros, in_specs, outs, scratch=()):
    return pl.pallas_call(
        kernel,
        name=name,
        in_specs=in_specs,
        out_specs=[VM] * len(outs),
        cost_estimate=cost(micros),
        out_shape=[jax.ShapeDtypeStruct(s, F32) for s in outs],
        scratch_shapes=list(scratch),
        compiler_params=pltpu.CompilerParams(vmem_limit_bytes=VMEM_LIMIT),
    )


def chunks(body):
    def step(k, carry):
        body(pl.ds(pl.multiple_of(k * CHUNK, CHUNK), CHUNK))
        return carry

    lax.fori_loop(0, ROWS // CHUNK, step, 0)


def pack_kernel(diag, off, schmid, crss, branch, rate, low, high, coef):
    for i in range(6):
        for j in range(6):
            k = 6 * i + j
            v = off[k] + diag[i] if i == j else off[k]
            coef[k] = v
            if k < HALF:
                low[k] = v
            else:
                high[k - HALF] = v
    bits = branch[...]
    speed = rate[...]
    for a in range(SLIP):
        limit = crss[a]
        inverse = 1.0 / limit
        for j in range(6):
            coef[36 + 6 * a + j] = schmid[6 * a + j] * inverse
        active = (jnp.right_shift(bits, a) & 1).astype(F32)
        coef[108 + a] = active * speed * (limit * limit)


def in_hbm(*arrays):
    return [pltpu.with_memory_space_constraint(v, pltpu.HBM) for v in arrays]


def pack(operands, planes, rows):
    block = lambda n: pl.BlockSpec((n, rows, LANES), lambda k: (0, k, 0))
    return pl.pallas_call(
        pack_kernel,
        name="pack",
        cost_estimate=cost(4),
        grid=(ROWS // rows,),
        in_specs=[
            block(v.shape[0]) if v.ndim == 3 else pl.BlockSpec((rows, LANES), lambda k: (k, 0))
            for v in operands
        ],
        out_specs=[block(n) for n in planes],
        out_shape=[jax.ShapeDtypeStruct((n, ROWS, LANES), F32) for n in planes],
        compiler_params=pltpu.CompilerParams(vmem_limit_bytes=VMEM_LIMIT),
    )(*in_hbm(*operands))


def times(c, at, vectors):
    sums = [[None] * 6 for _ in vectors]
    for i in range(6):
        for j in range(6):
            entry = c(6 * i + j, at)
            for s, vector in enumerate(vectors):
                term = entry * vector[j]
                sums[s][i] = term if j == 0 else sums[s][i] + term
    return sums


def load(ref, at):
    return [[ref[6 * s + i, at, :] for i in range(6)] for s in range(SLOTS)]


def store(ref, at, values):
    for s in range(SLOTS):
        for i in range(6):
            ref[6 * s + i, at, :] = values[s][i]


def slip(c, at, stress, total):
    total = [list(t) for t in total]
    for a in range(SLIP):
        rows = [c(36 + 6 * a + j, at) for j in range(6)]
        gain = c(108 + a, at)
        for s in range(SLOTS):
            t = rows[0] * stress[s][0]
            for j in range(1, 6):
                t = t + rows[j] * stress[s][j]
            w = gain * (t - jnp.tanh(t))
            for j in range(6):
                total[s][j] = total[s][j] - rows[j] * w
    return total


def around(x):
    rows = pltpu.roll(x, 1, axis=0) + pltpu.roll(x, ROWS - 1, axis=0)
    return rows + (pltpu.roll(x, 1, axis=1) + pltpu.roll(x, LANES - 1, axis=1))


def beside(sig_0, sig_1, base_0, base_1):
    def step(k, carry):
        for f in [k * GROUP + j for j in range(GROUP)]:
            u = sig_0[f]
            v = sig_1[f]
            base_0[f] = base_0[f] + SHARE * (around(u) + v)
            base_1[f] = base_1[f] + SHARE * (around(v) + u)
        return carry

    lax.fori_loop(0, FIELDS // GROUP, step, 0)


def combine(x, y, fn):
    return [[fn(x[s][i], y[s][i]) for i in range(6)] for s in range(SLOTS)]


def relaxed(e, sig):
    return combine(e, sig, lambda u, v: u - RELAX * v)


def whole(ref):
    return lambda k, at: ref[k, at, :]


def split(side, coefficients, run):
    own, other, near, far, rest = coefficients
    early = lambda k, at: near[k, at, :] if k < HALF else rest[k, at, :]
    late = lambda k, at: rest[k, at, :] if k < HALF else far[k - HALF, at, :]
    pl.when(side[0] == 0)(lambda: run(whole(own), whole(other), early, late))
    pl.when(side[0] == 1)(lambda: run(whole(other), whole(own), late, early))


def zero_kernel(side, ebar, own_hbm, other_hbm, own, other, *refs):
    t_0, t_1, sems = refs[2:]
    copies = [
        pltpu.make_async_copy(src.at[low:high], dst.at[low:high], sems.at[k])
        for k, (src, dst, low, high) in enumerate(
            (
                (own_hbm, own, 0, 36),
                (other_hbm, other, 0, 36),
                (own_hbm, own, 36, 120),
                (other_hbm, other, 36, 120),
            )
        )
    ]
    for copy in copies:
        copy.start()
    copies[0].wait()
    copies[1].wait()
    ready = lambda: (copies[2].wait(), copies[3].wait())
    zero_sweep(side, ebar, FIRST, own, other, *refs[:2], t_0, t_1, ready)


def entire_kernel(slot, side, ebar, own, other, near, far, rest, x_0, x_1, e_0, e_1, t_0, t_1):
    zero_sweep(side, ebar, slot, own, other, e_0, e_1, t_0, t_1, lambda: None)
    first_kernel(slot, side, ebar, own, other, near, far, rest, e_0, e_1, x_0, x_1)


def zero_sweep(side, ebar, slot, own, other, e_0, e_1, t_0, t_1, ready):
    def start(c_0, c_1):
        for c, t_ref, e_ref in ((c_0, t_0, e_0), (c_1, t_1, e_1)):

            def body(at, c=c, t_ref=t_ref, e_ref=e_ref):
                strain = uniform(ebar, slot)
                sig = times(c, at, strain)
                store(t_ref, at, sig)
                store(e_ref, at, relaxed(strain, sig))

            chunks(body)

    def end(c_0, c_1):
        for c, t_ref, e_ref in ((c_0, t_0, e_0), (c_1, t_1, e_1)):

            def body(at, c=c, t_ref=t_ref, e_ref=e_ref):
                store(e_ref, at, slip(c, at, load(t_ref, at), load(e_ref, at)))

            chunks(body)

    ordered(side, own, other, start)
    beside(t_0, t_1, e_0, e_1)
    ready()
    ordered(side, own, other, end)


def ordered(side, own, other, run):
    pl.when(side[0] == 0)(lambda: run(whole(own), whole(other)))
    pl.when(side[0] == 1)(lambda: run(whole(other), whole(own)))


def uniform(ebar, k):
    return [[jnp.full((CHUNK, LANES), ebar[k, i], F32) for i in range(6)]]


def first_kernel(slot, side, ebar, own, other, near, far, rest, e_0, e_1, x_0, x_1):
    def run(c_0, c_1, g_0, g_1):
        for c, g, e_ref, x_ref in ((c_0, g_0, e_0, x_0), (c_1, g_1, e_1, x_1)):

            def body(at, c=c, g=g, e_ref=e_ref, x_ref=x_ref):
                outer = times(g, at, uniform(ebar, slot))
                e = combine(load(e_ref, at), outer, lambda u, v: u + SHARE * v)
                onward(c, at, e, x_ref)

            chunks(body)

    split(side, (own, other, near, far, rest), run)
    beside_own(x_0, x_1)


def onward(c, at, e, x_ref):
    sig = times(c, at, e)
    store(x_ref.at[0:FIELDS], at, sig)
    store(x_ref.at[FIELDS:], at, slip(c, at, sig, relaxed(e, sig)))


def advance(planes):
    for c, t_ref, e_ref, x_ref in planes:

        def body(at, c=c, t_ref=t_ref, e_ref=e_ref, x_ref=x_ref):
            onward(c, at, slip(c, at, load(t_ref, at), load(e_ref, at)), x_ref)

        chunks(body)


def beside_own(x_0, x_1):
    beside(x_0.at[0:FIELDS], x_1.at[0:FIELDS], x_0.at[FIELDS:], x_1.at[FIELDS:])


def arrive(planes):
    for x_ref, far_ref, c, g, t_ref, e_ref in planes:

        def body(at, x_ref=x_ref, far_ref=far_ref, c=c, g=g, t_ref=t_ref, e_ref=e_ref):
            add = lambda u, v: u + SHARE * v
            own = x_ref.at[0:FIELDS], x_ref.at[FIELDS:]
            far = far_ref.at[0:FIELDS], far_ref.at[FIELDS:]
            e = combine(load(own[1], at), load(far[0], at), add)
            sig = times(c, at, e)
            store(t_ref, at, sig)
            base = relaxed(e, sig)
            outer = times(g, at, combine(load(far[1], at), load(own[0], at), add))
            store(e_ref, at, combine(base, outer, add))

        chunks(body)


def two_sweeps(c_0, c_1, g_0, g_1, x_0, x_1, f_0, f_1, y_0, y_1, e_0, e_1, t_0, t_1):
    arrive(((x_0, f_0, c_0, g_0, t_0, e_0), (x_1, f_1, c_1, g_1, t_1, e_1)))
    beside(t_0, t_1, e_0, e_1)
    advance(((c_0, t_0, e_0, y_0), (c_1, t_1, e_1, y_1)))
    beside_own(y_0, y_1)


def pair_kernel(side, own, other, near, far, rest, *refs):
    split(side, (own, other, near, far, rest), lambda *c: two_sweeps(*c, *refs))


def last_kernel(side, own, other, near, far, rest, x_0, x_1, f_0, f_1, out, y_0, y_1, *temps):
    def run(c_0, c_1, g_0, g_1):
        two_sweeps(c_0, c_1, g_0, g_1, x_0, x_1, f_0, f_1, y_0, y_1, *temps)
        for k in range(FIELDS):
            out[k] = jnp.zeros((CHUNK, LANES), F32)
        for y_ref, c, g in ((y_0, c_0, g_0), (y_1, c_1, g_1)):

            def body(at, y_ref=y_ref, c=c, g=g):
                mine = times(c, at, load(y_ref.at[FIELDS:], at))
                outer = times(g, at, load(y_ref.at[0:FIELDS], at))
                for s in range(SLOTS):
                    for i in range(6):
                        out[6 * s + i] = out[6 * s + i] + (mine[s][i] + SHARE * outer[s][i])

            chunks(body)

    split(side, (own, other, near, far, rest), run)


def strain_kernel(node, owner, member, disp, before, after, out, grid):
    grid[:, 0:1] = before[...]
    grid[:, 1:3] = disp[...]
    grid[:, 3:4] = after[...]
    lane = lax.broadcasted_iota(jnp.int32, (1, LANES), 1)
    group = lax.broadcasted_iota(jnp.int32, (8, LANES), 0)
    total = jnp.zeros((8, LANES), F32)
    for p in range(2):
        local = node[p] - member[0] * (2 * 32 * LANES)
        present = (local >= 0) & (local < 2 * 32 * LANES)
        local = jnp.clip(local, 0, 2 * 32 * LANES - 1)
        x = local // (32 * LANES)
        y = (local // LANES) % 32
        z = local % LANES
        up_y = jnp.minimum(y + 1, 31)
        down_y = jnp.maximum(y - 1, 0)
        has_up = jnp.where(y < 31, 1.0, 0.0).astype(F32)
        has_down = jnp.where(y > 0, 1.0, 0.0).astype(F32)
        slope = []
        for c in range(3):
            row = lambda dx, yy: grid[c, x + dx, pl.ds(yy, 1), :]
            gx = (row(2, y) - row(0, y)) * 0.5
            gy = (row(1, up_y) * has_up - row(1, down_y) * has_down) * 0.5
            mid = row(1, y)
            right = jnp.where(lane < LANES - 1, pltpu.roll(mid, LANES - 1, axis=1), 0.0)
            left = jnp.where(lane > 0, pltpu.roll(mid, 1, axis=1), 0.0)
            slope.append((gx, gy, (right - left) * 0.5))
        parts = [
            slope[0][0],
            slope[1][1],
            slope[2][2],
            slope[1][2] + slope[2][1],
            slope[0][2] + slope[2][0],
            slope[0][1] + slope[1][0],
        ]
        here = (lane == z) & present
        line = jnp.zeros((1, LANES), F32)
        for j, part in enumerate(parts):
            value = jnp.sum(jnp.where(here, part, 0.0), axis=1, keepdims=True)
            line = line + jnp.where(lane == j, value, 0.0)
        total = total + jnp.where(group == owner[p, 0], line, 0.0)
    out[...] = total


def stencil_kernel(blocks, disp, before, after, external, out, moved, total):
    step = pl.program_id(0)

    @pl.when(step == 0)
    def _():
        lane = lax.broadcasted_iota(jnp.int32, (32, LANES), 1)
        row = lax.broadcasted_iota(jnp.int32, (32, LANES), 0)
        total[...] = jnp.zeros_like(total)
        for c in range(3):
            for x in range(4):
                v = before[c, 0] if x == 0 else (after[c, 0] if x == 3 else disp[c, x - 1])
                for j in range(3):
                    w = v
                    if j == 0:
                        w = jnp.where(row > 0, pltpu.roll(v, 1, axis=0), 0.0)
                    if j == 2:
                        w = jnp.where(row < 31, pltpu.roll(v, 31, axis=0), 0.0)
                    moved[j, 0, c, x] = jnp.where(lane > 0, pltpu.roll(w, 1, axis=1), 0.0)
                    moved[j, 1, c, x] = w
                    moved[j, 2, c, x] = jnp.where(lane < LANES - 1, pltpu.roll(w, LANES - 1, axis=1), 0.0)

    i = step // 3
    j = step % 3
    for c in range(3):
        for x in range(2):
            s = total[c, x]
            for k in range(3):
                for d in range(3):
                    s = s + blocks[k, c, d, x].astype(F32) * moved[j, k, d, i + x]
            total[c, x] = s

    @pl.when(step == 8)
    def _():
        out[...] = external[...] - total[...]


def stencil(stiffness, disp, before, after, external):
    whole = lambda n: pl.BlockSpec((3, n, 32, LANES), lambda s: (0, 0, 0, 0))
    return pl.pallas_call(
        stencil_kernel,
        name="stencil",
        cost_estimate=cost(5),
        grid=(9,),
        in_specs=[
            pl.BlockSpec((3, 3, 3, 2, 32, LANES), lambda s: (s, 0, 0, 0, 0, 0)),
            whole(2),
            whole(1),
            whole(1),
            whole(2),
        ],
        out_specs=whole(2),
        out_shape=jax.ShapeDtypeStruct((3, 2, 32, LANES), F32),
        scratch_shapes=[
            pltpu.VMEM((3, 3, 3, 4, 32, LANES), F32),
            pltpu.VMEM((3, 2, 32, LANES), F32),
        ],
        compiler_params=pltpu.CompilerParams(vmem_limit_bytes=VMEM_LIMIT),
    )(*in_hbm(stiffness, disp, before, after, external))


def final_kernel(node, owner, member, received, loads, base, residual, stress):
    residual[...] = base[...]
    lane = lax.broadcasted_iota(jnp.int32, (1, LANES), 1)
    sums = [jnp.sum(received[g], axis=0, keepdims=True) for g in range(4)]
    for p in range(2):
        line = jnp.zeros((1, LANES), F32)
        for g in range(4):
            line = line + jnp.where(owner[p, 0] == g, sums[g], 0.0)
        line = line * (1.0 / 262144.0)
        stress[p : p + 1, :] = line[:, 0:6]
        local = node[p] - member[0] * (2 * 32 * LANES)
        present = (local >= 0) & (local < 2 * 32 * LANES)
        local = jnp.clip(local, 0, 2 * 32 * LANES - 1)
        x = local // (32 * LANES)
        y = (local // LANES) % 32
        z = local % LANES
        here = (lane == z) & present
        for c in range(3):
            force = jnp.sum(loads[p, c : c + 1, :] * line, axis=1, keepdims=True)
            row = residual[c, x, pl.ds(y, 1), :]
            residual[c, x, pl.ds(y, 1), :] = row - jnp.where(here, force, 0.0)


def per_device(
    displacement,
    stiffness,
    external,
    point_node,
    point_owner,
    point_load,
    moduli_diag,
    moduli_off,
    schmid,
    crss,
    branch,
    rate,
):
    groups = lax.axis_size("grp")
    members = lax.axis_size("rve")
    member = lax.axis_index("rve")
    everyone = groups * members

    def over(value, pairs, axis="rve"):
        return lax.ppermute(value, axis, pairs)

    partner = [(i, i ^ 1) for i in range(members)]
    across = [(i, (i - 1 if i % 2 == 0 else i + 1) % members) for i in range(members)]
    along = [(i, (i - 2 if i % 2 == 0 else i + 2) % members) for i in range(members)]
    rightward = [(i, (i + 2) % members) for i in range(members)]
    leftward = [(i, (i - 2) % members) for i in range(members)]

    both = ("grp", "rve")
    upward = [(i, i + 1) for i in range(everyone - 1)]
    downward = [(i + 1, i) for i in range(everyone - 1)]
    before = over(displacement[:, 1:2], upward, both)
    after = over(displacement[:, 0:1], downward, both)

    low, high, own = pack(
        (moduli_diag[0, :, 0], moduli_off[0, :, 0], schmid[0, :, 0], crss[0, :, 0], branch[0, 0], rate[0, 0]),
        (HALF, HALF, 120),
        32,
    )
    before, after, low, high, own = lax.optimization_barrier((before, after, low, high, own))
    near = over(low, across)
    far = over(high, along)
    other = over(own, partner)
    core = member % 2

    where = member.reshape(1).astype(jnp.int32)
    message = call(
        strain_kernel,
        "strain",
        0.1,
        [SM, SM, SM, VM, VM, VM],
        [(8, LANES)],
        [pltpu.VMEM((3, 4, 32, LANES), F32)],
    )(point_node, point_owner, where, displacement, before, after)[0]
    message = jnp.broadcast_to(message[:groups, None, None, :], (groups, members, 1, LANES))
    arrived = lax.all_to_all(message.reshape(everyone, 1, LANES), both, 0, 0, tiled=True)
    near, far, arrived = lax.optimization_barrier((near, far, arrived))
    rest = over(jnp.concatenate([near, far], axis=0), partner)
    strains = jnp.sum(arrived.reshape(groups, members, LANES), axis=1)
    ebar = lax.dynamic_slice_in_dim(strains, core * PER_CORE, PER_CORE, axis=0)

    base = stencil(stiffness, displacement, before, after, external)

    plane = (FIELDS, ROWS, LANES)
    packed = (2 * FIELDS, ROWS, LANES)
    temps = [pltpu.VMEM(plane, F32)] * 4
    side = core.reshape(1).astype(jnp.int32)
    ghosts = (near, far, rest)
    ANY = pl.BlockSpec(memory_space=pl.ANY)
    outs = call(
        zero_kernel,
        "zero",
        5,
        [SM] * 2 + [ANY] * 2,
        [(120, ROWS, LANES)] * 2 + [plane] * 2,
        temps[:2] + [pltpu.SemaphoreType.DMA((4,))],
    )(side, ebar, *in_hbm(own, other))
    fixed = (*outs[:2], *ghosts)
    state = [None] * PER_CORE
    for k in range(PER_CORE):
        if k == FIRST:
            kernel = functools.partial(first_kernel, k)
            state[k] = call(kernel, "first", 5, [SM] * 2 + [VM] * 7, [packed] * 2)(side, ebar, *fixed, *outs[2:])
        else:
            kernel = functools.partial(entire_kernel, k)
            state[k] = call(kernel, "entire", 5, [SM] * 2 + [VM] * 5, [packed] * 2, temps)(side, ebar, *fixed)
    sums = []
    for pair in range(4):
        for k in range(PER_CORE):
            x_0, x_1 = state[k]
            f_0 = over(x_1, rightward)
            f_1 = over(x_0, leftward)
            operands = (side, *fixed, x_0, x_1, f_0, f_1)
            if pair < 3:
                state[k] = call(pair_kernel, "pair", 5, [SM] + [VM] * 9, [packed] * 2, temps)(*operands)
            else:
                sizes = [pltpu.VMEM(packed, F32)] * 2 + temps
                sums += call(last_kernel, "last", 6, [SM] + [VM] * 9, [(FIELDS, CHUNK, LANES)], sizes)(*operands)

    totals = jnp.stack([jnp.sum(v, axis=(1, 2)) for v in lax.optimization_barrier(sums)])
    totals = jnp.pad(totals, ((0, 0), (0, LANES - 6)))
    mine = jnp.zeros((groups, LANES), F32)
    mine = lax.dynamic_update_slice_in_dim(mine, totals, core * PER_CORE, axis=0)
    reply = jnp.broadcast_to(mine[:, None, None, :], (groups, members, 1, LANES))
    received = lax.all_to_all(reply.reshape(everyone, 1, LANES), both, 0, 0, tiled=True)
    loads = jnp.pad(point_load.reshape(-1, 3, 6), ((0, 0), (0, 0), (0, LANES - 6)))
    residual, point_stress = call(
        final_kernel, "final", 2, [SM, SM, SM, VM, VM, VM], [(3, 2, 32, LANES), (2, 6)]
    )(point_node, point_owner, where, received.reshape(groups, members, LANES), loads, base)
    return (residual, point_stress)


def solution(mesh):
    in_specs = (
        P(None, ("grp", "rve"), None, None),
        P(None, None, None, ("grp", "rve"), None, None),
        P(None, ("grp", "rve"), None, None),
        P("grp"),
        P("grp", None),
        P("grp", None),
        P("grp", None, "rve", None, None),
        P("grp", None, "rve", None, None),
        P("grp", None, "rve", None, None),
        P("grp", None, "rve", None, None),
        P("grp", "rve", None, None),
        P("grp", "rve", None, None),
    )
    out_specs = (P(None, ("grp", "rve"), None, None), P("grp", None))
    return jax.shard_map(
        per_device, mesh=mesh, in_specs=in_specs, out_specs=out_specs, check_vma=False
    )
```
